32 devices in a mesh: groups: 2 (over x), blk: 16 (over z, y, core).
Axes of the slice: x: 2, y: 2, z: 4, core: 2. Of those that a mesh axis runs over, the one named last changes fastest.
Arguments:
- traces: bfloat16 [8192, 12000], P(('groups', 'blk')), parts along dimension 0
- record_id: int32 [8192], P(('groups', 'blk')), parts along dimension 0, may hold values from 0 to 4095, as said below
Outputs:
- correlations: bfloat16 [1024, 4, 32, 801], P(('groups', 'blk')), parts along dimension 0
The draws below stay inside these ranges and needn't reach their ends.
There are 2 independent parts, one for each index of `groups`. The reference program is written for one: setup_inputs(seed, part) draws one part's arguments, and reference() takes and returns one part's arrays. A program takes and returns all parts, laid end to end along the dimension named above; each array names one. Nothing has to cross between parts.
Inputs may be any that keep to these rules, and one draw needn't show every extreme that they name: `record_id`: every value appears exactly once among one part's records; value v is channel v // 8 in window v mod 8. The records of one index of blk hold at most 32 of one owner's records (owner = v // 256), some index holds exactly 32 records for some owner in every draw, and every owner's 256 records come from the devices together.
All inputs are finite; a program needn't handle non-finite values.
Results may differ from the reference program's by a relative error of at most 0.0075.
Values may be sent and summed in bfloat16 or wider, within the bound.
No kernel may reach another device: no remote copies, remote signals or barrier semaphores. Data moves between devices by JAX's collectives and lax.ppermute only.
A program may use at most 192 MiB of HBM per device.

```python
import math
import jax
import jax.numpy as jnp
from jax import lax

CH_DEV = 32
NWIN = 8
WS = 12000
F = 512
LOWBIN = 60
LAG = 400
HOPS = 3
RECS = 256
N_BLK = 16


def draw_traces(key, part):
    row_total = N_BLK * RECS
    key_gain, key_base = jax.random.split(key, 2)
    row_gain = jnp.exp(jax.random.uniform(key_gain, (row_total, 1), jnp.float32, 0.0, math.log(10.0)))
    values = jax.random.normal(key_base, (row_total, WS), jnp.float32) * row_gain
    return values.astype(jnp.bfloat16)


def draw_record_id(key, part):
    peer_count = N_BLK
    rec_count = RECS
    capacity = 2 * rec_count // peer_count
    key_load, key_order, key_rows, key_cols, key_perm, key_shuffle = jax.random.split(key, 6)
    pair_first = jax.random.randint(key_load, (peer_count // 2,), 0, capacity + 1).at[0].set(capacity)
    pair_load = jnp.concatenate([pair_first, capacity - pair_first])
    pair_load = pair_load[jax.random.permutation(key_order, peer_count)]
    row_perm = jax.random.permutation(key_rows, peer_count)
    col_perm = jax.random.permutation(key_cols, peer_count)
    counts = pair_load[(col_perm[None, :] - row_perm[:, None]) % peer_count]
    cum_incl = jnp.cumsum(counts, axis=0)
    col_start = cum_incl - counts
    row_start = jnp.cumsum(counts, axis=1) - counts
    record_pos = jnp.arange(rec_count, dtype=jnp.int32)
    source = jnp.sum((cum_incl.T[:, :, None] <= record_pos[None, None, :]).astype(jnp.int32), axis=1)
    owner_col = jnp.arange(peer_count, dtype=jnp.int32)[:, None]
    position = row_start[source, owner_col] + record_pos[None, :] - col_start[source, owner_col]
    perm_keys = jax.random.split(key_perm, peer_count)
    owner_perm = jax.vmap(lambda one_key: jax.random.permutation(one_key, rec_count))(perm_keys)
    id_values = owner_col * rec_count + owner_perm
    flat_index = (source * rec_count + position).reshape(-1)
    placed = jnp.zeros((peer_count * rec_count,), jnp.int32).at[flat_index].set(id_values.reshape(-1).astype(jnp.int32))
    shuffle_keys = jax.random.split(key_shuffle, peer_count)
    shuffled = jax.vmap(lambda one_key, row_values: row_values[jax.random.permutation(one_key, rec_count)])(shuffle_keys, placed.reshape(peer_count, rec_count))
    return shuffled.reshape(-1).astype(jnp.int32)


def setup_inputs(seed: int = 0, part: int = 0) -> dict:
    key_of = jax.random.split(jax.random.key(seed), 3)
    part_splits = jax.random.split(jax.random.fold_in(key_of[2], part), 3)
    return {
        "traces": draw_traces(jax.random.fold_in(jax.random.fold_in(key_of[2], part), 71), part),
        "record_id": draw_record_id(jax.random.fold_in(jax.random.fold_in(key_of[2], part), 71), part),
    }


def forward_table():
    sample_index = jnp.arange(WS, dtype=jnp.int32)[:, None]
    bin_index = LOWBIN + jnp.arange(F, dtype=jnp.int32)[None, :]
    residue = (sample_index * bin_index % WS).astype(jnp.float32)
    angles = 2.0 * math.pi / WS * residue
    table = jnp.concatenate([jnp.cos(angles), -jnp.sin(angles)], axis=1)
    return table.astype(jnp.bfloat16)

def inverse_table():
    bin_index = LOWBIN + jnp.arange(F, dtype=jnp.int32)[:, None]
    lag_index = jnp.arange(2 * LAG + 1, dtype=jnp.int32)[None, :] - LAG + WS
    residue = (bin_index * lag_index % WS).astype(jnp.float32)
    angles = 2.0 * math.pi / WS * residue
    table = jnp.concatenate([jnp.cos(angles), -jnp.sin(angles)], axis=0)
    return table.astype(jnp.bfloat16)

def whiten(row_block, forward):
    spectrum = jnp.dot(row_block, forward, preferred_element_type=jnp.float32)
    power_mean = lax.optimization_barrier(jnp.sum(spectrum * spectrum, axis=1, keepdims=True)) / F
    return (spectrum * lax.rsqrt(power_mean + 1e-06)).astype(jnp.bfloat16)

def correlate(left_panel, right_panel, inverse, hop_index):
    left_real = left_panel[:, :, :F].astype(jnp.float32)
    left_imag = left_panel[:, :, F:].astype(jnp.float32)
    right_real = right_panel[:, :, :F].astype(jnp.float32)
    right_imag = right_panel[:, :, F:].astype(jnp.float32)
    cross_real = jnp.einsum('cwk,ewk->cek', left_real, right_real) + jnp.einsum('cwk,ewk->cek', left_imag, right_imag)
    cross_imag = jnp.einsum('cwk,ewk->cek', left_imag, right_real) - jnp.einsum('cwk,ewk->cek', left_real, right_imag)
    cross = jnp.concatenate([cross_real, cross_imag], axis=2).astype(jnp.bfloat16)
    width = left_panel.shape[0]
    lagged = jnp.dot(cross.reshape(width * width, 2 * F), inverse, preferred_element_type=jnp.float32)
    lagged = lagged.reshape(width, width, 2 * LAG + 1) * (1.0 / math.sqrt(F * NWIN))
    if hop_index == 0:
        self_pair = jnp.arange(width)[:, None] == jnp.arange(width)[None, :]
        lagged = jnp.where(self_pair[:, :, None], jnp.float32(0.0), lagged)
    return lagged.astype(jnp.bfloat16)

def reference(traces, record_id):
    forward = forward_table()
    total_rows = traces.shape[0]
    blocks = traces.reshape(total_rows // RECS, RECS, WS)
    spectra = lax.map(lambda row_block: whiten(row_block, forward), blocks).reshape(total_rows, 2 * F)
    ordered = jnp.zeros((total_rows, 2 * F), jnp.bfloat16).at[record_id.astype(jnp.int32)].set(spectra)
    panels = ordered.reshape(N_BLK, CH_DEV, NWIN, 2 * F)
    inverse = inverse_table()

    def one_block(block_index):
        own_panel = lax.dynamic_index_in_dim(panels, block_index, 0, keepdims=False)
        per_hop = []
        for hop_index in range(HOPS + 1):
            partner = lax.dynamic_index_in_dim(panels, ((block_index + hop_index) % N_BLK).astype(jnp.int32), 0, keepdims=False)
            per_hop.append(correlate(own_panel, partner, inverse, hop_index))
        return jnp.stack(per_hop, axis=1)
    result = lax.map(one_block, jnp.arange(N_BLK, dtype=jnp.int32))
    return result.reshape(N_BLK * CH_DEV, HOPS + 1, CH_DEV, 2 * LAG + 1)
```

```python
import functools
import math

import jax
import jax.numpy as jnp
import numpy as np
from jax import lax
from jax.experimental import pallas as pl
from jax.experimental.pallas import tpu as pltpu
from jax.sharding import PartitionSpec as P

NWIN = 8
WS = 12000
F = 512
LOWBIN = 60
LAG = 400
HOPS = 3
NLAG = 2 * LAG + 1
HALF = WS // 2
CHUNK = 240
STEPS = HALF // CHUNK
KPAD = 256
BINS = LOWBIN + np.concatenate([np.arange(0, F, 2), np.arange(1, F, 2)])
VMEM_LIMIT = 56 * 1024 * 1024


def shifted(block, axis, distance):
    devices = range(lax.axis_size(axis))
    route = [((i - distance) % len(devices), i) for i in devices]
    return lax.ppermute(block, axis, route)


def inverse_table():
    bin_index = jnp.asarray(BINS, jnp.int32)[:, None]
    lag_index = jnp.arange(NLAG, dtype=jnp.int32)[None, :] - LAG + WS
    residue = (bin_index * lag_index % WS).astype(jnp.float32)
    angles = 2.0 * math.pi / WS * residue
    table = jnp.concatenate([jnp.cos(angles), -jnp.sin(angles)], axis=0)
    return table.astype(jnp.bfloat16)


def forward_start():
    angles = 2.0 * np.pi / WS * (BINS[:, None] * np.arange(CHUNK)[None, :] % WS)
    start = np.zeros((2, F, KPAD), np.float32)
    start[0, :, :CHUNK] = np.cos(angles)
    start[1, :, :CHUNK] = -np.sin(angles)
    step = 2.0 * np.pi / WS * (BINS * CHUNK % WS)
    turn = np.stack([np.cos(step), -np.sin(step)]).astype(np.float32)
    return start, np.ascontiguousarray(np.broadcast_to(turn[:, :, None], (2, F, 128)))


def label_kernel(capacity, rec_count, id_ref, target_ref, label_ref):
    ids = id_ref[...]
    slots = label_ref.shape[1]
    owner = ids // rec_count
    row = jnp.broadcast_to(owner, (rec_count, rec_count))
    col = row.T
    before = lax.broadcasted_iota(jnp.int32, row.shape, 0) < lax.broadcasted_iota(
        jnp.int32, row.shape, 1
    )
    same = jnp.where((row == col) & before, 1, 0)
    rank = jnp.sum(same, axis=0, keepdims=True)
    target = owner * capacity + rank
    target_ref[...] = target
    packed = jnp.broadcast_to(target, (128, rec_count)).T
    id_col = jnp.broadcast_to(ids, (128, rec_count)).T
    for part in range(slots // 128):
        lane = lax.broadcasted_iota(jnp.int32, packed.shape, 1) + part * 128
        hit = jnp.where(packed == lane, id_col + 1, 0)
        label_ref[:, part * 128 : (part + 1) * 128] = jnp.sum(hit, axis=0, keepdims=True) - 1


def make_labels(record_id, peer_count, capacity):
    rec_count = record_id.shape[0]
    slots = peer_count * capacity
    return pl.pallas_call(
        functools.partial(label_kernel, capacity, rec_count),
        out_shape=(
            jax.ShapeDtypeStruct((1, rec_count), jnp.int32),
            jax.ShapeDtypeStruct((1, slots), jnp.int32),
        ),
        name="labels",
    )(record_id.reshape(1, rec_count))


def spectrum_kernel(target_ref, x0_ref, x1_ref, start_ref, turn_ref, out_ref, state, table, sums, acc):
    step = pl.program_id(0)

    @pl.when(step == 0)
    def _():
        state[...] = start_ref[...]
        sums[...] = jnp.zeros_like(sums)
        acc[...] = jnp.zeros_like(acc)

    half = F // 2
    block = 64
    for row in range(0, F, block):
        rows = slice(row, row + block)
        real = state[0, rows, :]
        imag = state[1, rows, :]
        base = row if row < half else row + half
        table[base : base + block, :] = real.astype(jnp.bfloat16)
        table[base + half : base + half + block, :] = imag.astype(jnp.bfloat16)
        turn_real = jnp.concatenate([turn_ref[0, rows, :]] * 2, axis=1)
        turn_imag = jnp.concatenate([turn_ref[1, rows, :]] * 2, axis=1)
        state[0, rows, :] = real * turn_real - imag * turn_imag
        state[1, rows, :] = real * turn_imag + imag * turn_real
    sums[0, :CHUNK, :] = x0_ref[...] + x1_ref[...]
    sums[1, :CHUNK, :] = x0_ref[...] - x1_ref[...]
    acc[:F, :] += jnp.dot(table[:F, :], sums[0], preferred_element_type=jnp.float32)
    acc[F:, :] += jnp.dot(table[F:, :], sums[1], preferred_element_type=jnp.float32)

    @pl.when(step == STEPS - 1)
    def _():
        power = jnp.sum(acc[...] * acc[...], axis=0, keepdims=True) / F
        scale = lax.rsqrt(power + 1e-06)
        slot = lax.broadcasted_iota(jnp.int32, (out_ref.shape[0], target_ref.shape[1]), 0)
        pick = jnp.where(slot == target_ref[...], 1.0, 0.0).astype(jnp.bfloat16)
        for place, row in enumerate((0, F, half, F + half)):
            white = (acc[row : row + half, :] * scale).astype(jnp.bfloat16)
            out_ref[:, place * half : (place + 1) * half] = lax.dot_general(
                pick, white, (((1,), (1,)), ((), ())), preferred_element_type=jnp.float32
            ).astype(jnp.bfloat16)


def spectra(traces, target, slots):
    rec_count = traces.shape[0]
    start, turn = forward_start()
    lanes = traces.T
    return pl.pallas_call(
        spectrum_kernel,
        grid=(STEPS,),
        in_specs=[
            pl.BlockSpec((1, rec_count), lambda i: (0, 0)),
            pl.BlockSpec((CHUNK, rec_count), lambda i: (i, 0)),
            pl.BlockSpec((CHUNK, rec_count), lambda i: (i + STEPS, 0)),
            pl.BlockSpec((2, F, KPAD), lambda i: (0, 0, 0)),
            pl.BlockSpec((2, F, 128), lambda i: (0, 0, 0)),
        ],
        out_specs=pl.BlockSpec((slots, 2 * F), lambda i: (0, 0)),
        out_shape=jax.ShapeDtypeStruct((slots, 2 * F), jnp.bfloat16),
        scratch_shapes=[
            pltpu.VMEM((2, F, KPAD), jnp.float32),
            pltpu.VMEM((2 * F, KPAD), jnp.bfloat16),
            pltpu.VMEM((2, KPAD, rec_count), jnp.bfloat16),
            pltpu.VMEM((2 * F, rec_count), jnp.float32),
        ],
        compiler_params=pltpu.CompilerParams(vmem_limit_bytes=VMEM_LIMIT),
        cost_estimate=pl.CostEstimate(
            flops=2 * rec_count * WS * F, bytes_accessed=2 * rec_count * WS, transcendentals=0
        ),
        name="spectra",
    )(target, lanes, lanes, jnp.asarray(start), jnp.asarray(turn))


def place_kernel(rec_count, label_ref, arrived_ref, out_ref):
    label = label_ref[...]
    local = label % rec_count
    row = jnp.where(label >= 0, local % NWIN * (rec_count // NWIN) + local // NWIN, -1)
    want = lax.broadcasted_iota(jnp.int32, (rec_count, label.shape[1]), 0)
    pick = jnp.where(want == row, 1.0, 0.0).astype(jnp.bfloat16)
    out_ref[...] = jnp.dot(pick, arrived_ref[...], preferred_element_type=jnp.float32).astype(
        jnp.bfloat16
    )


def place(labels, arrived, rec_count):
    return pl.pallas_call(
        functools.partial(place_kernel, rec_count),
        out_shape=jax.ShapeDtypeStruct((rec_count, 2 * F), jnp.bfloat16),
        compiler_params=pltpu.CompilerParams(vmem_limit_bytes=VMEM_LIMIT),
        name="place",
    )(labels, arrived)


def correlate_kernel(hop_index, group, *refs):
    own_ref, other_ref, inverse_ref = refs[:3]
    out_ref, mine, theirs, cross = refs[-4:]
    width = own_ref.shape[0] // NWIN
    step = pl.program_id(0)

    @pl.when(step == 0)
    def _():
        for w in range(NWIN):
            rows = slice(w * width, (w + 1) * width)
            real = own_ref[rows, :F].astype(jnp.float32)
            imag = own_ref[rows, F:].astype(jnp.float32)
            mine[0, rows, :] = real + imag
            mine[1, rows, :] = real
            mine[2, rows, :] = imag
            real = other_ref[rows, :F].astype(jnp.float32)
            imag = other_ref[rows, F:].astype(jnp.float32)
            theirs[0, rows, :] = real
            theirs[1, rows, :] = real + imag
            theirs[2, rows, :] = real - imag

    blocks = [
        pl.ds(pl.multiple_of(w * width + step * group, group), group) for w in range(NWIN)
    ]
    for tile in range(F // 128):
        lanes = slice(tile * 128, (tile + 1) * 128)
        for first in range(0, group, 2):
            total = [[None] * 3 for _ in range(2)]
            for w in range(NWIN):
                for j in range(3):
                    factor = theirs[j, w * width : (w + 1) * width, lanes]
                    rows = mine.at[j, blocks[w], lanes]
                    for c in range(2):
                        term = factor * rows[first + c : first + c + 1, :]
                        total[c][j] = term if w == 0 else total[c][j] + term
            for c in range(2):
                rows = slice((first + c) * width, (first + c + 1) * width)
                cross[rows, tile * 128 : (tile + 1) * 128] = (total[c][0] - total[c][2]).astype(
                    jnp.bfloat16
                )
                cross[rows, F + tile * 128 : F + (tile + 1) * 128] = (
                    total[c][0] - total[c][1]
                ).astype(jnp.bfloat16)
    lagged = jnp.dot(cross[...], inverse_ref[...], preferred_element_type=jnp.float32)
    lagged = (lagged * (1.0 / math.sqrt(F * NWIN))).reshape(group, width, NLAG)
    if hop_index == 0:
        shape = (group, width, NLAG)
        channel = lax.broadcasted_iota(jnp.int32, shape, 0) + step * group
        lagged = jnp.where(channel == lax.broadcasted_iota(jnp.int32, shape, 1), 0.0, lagged)
    out_ref[...] = lagged.astype(jnp.bfloat16)[:, None]


def correlate(own, other, inverse, hop_index, result):
    rec_count = own.shape[0]
    width = rec_count // NWIN
    group = 8
    whole = lambda shape: pl.BlockSpec(shape, lambda i: (0,) * len(shape))
    in_specs = [whole(own.shape), whole(other.shape), whole(inverse.shape)]
    operands = [own, other, inverse]
    aliases = {}
    if result is not None:
        in_specs.append(pl.BlockSpec(memory_space=pl.ANY))
        operands.append(result)
        aliases = {3: 0}
    pairs = width * width
    return pl.pallas_call(
        functools.partial(correlate_kernel, hop_index, group),
        grid=(width // group,),
        in_specs=in_specs,
        out_specs=pl.BlockSpec((group, 1, width, NLAG), lambda i: (i, hop_index, 0, 0)),
        out_shape=jax.ShapeDtypeStruct((width, HOPS + 1, width, NLAG), jnp.bfloat16),
        scratch_shapes=[
            pltpu.VMEM((3, rec_count, F), jnp.float32),
            pltpu.VMEM((3, rec_count, F), jnp.float32),
            pltpu.VMEM((group * width, 2 * F), jnp.bfloat16),
        ],
        input_output_aliases=aliases,
        compiler_params=pltpu.CompilerParams(vmem_limit_bytes=VMEM_LIMIT),
        cost_estimate=pl.CostEstimate(
            flops=pairs * 2 * F * NLAG * 4, bytes_accessed=pairs * NLAG * 2, transcendentals=0
        ),
        name="correlate",
    )(*operands)


def on_device(traces, record_id):
    rec_count = traces.shape[0]
    peer_count = lax.axis_size("blk")
    capacity = 2 * rec_count // peer_count
    slots = peer_count * capacity
    target, labels = make_labels(record_id, peer_count, capacity)
    labels = lax.all_to_all(
        labels.reshape(peer_count, 1, capacity), "blk", split_axis=0, concat_axis=0, tiled=True
    ).reshape(1, slots)
    outgoing = spectra(traces, target, slots).reshape(peer_count, capacity, 2 * F)
    arrived = lax.all_to_all(outgoing, "blk", split_axis=0, concat_axis=0, tiled=True)
    own = place(labels, arrived.reshape(slots, 2 * F), rec_count)
    inverse = inverse_table()
    result = None
    visiting = own
    for hop_index in range(HOPS + 1):
        if hop_index > 0:
            visiting = shifted(visiting, "blk", -1)
        result = correlate(own, visiting, inverse, hop_index, result)
    return result


def solution(mesh):
    return jax.shard_map(
        on_device,
        mesh=mesh,
        in_specs=(P(("groups", "blk"), None), P(("groups", "blk"))),
        out_specs=P(("groups", "blk"), None, None, None),
        check_vma=False,
    )
```

```python
import functools
import math

import jax
import jax.numpy as jnp
import numpy as np
from jax import lax
from jax.experimental import pallas as pl
from jax.experimental.pallas import tpu as pltpu
from jax.sharding import PartitionSpec as P

NWIN = 8
WS = 12000
F = 512
LOWBIN = 60
LAG = 400
HOPS = 3
NLAG = 2 * LAG + 1
HALF = WS // 2
CHUNK = 1200
STEPS = HALF // CHUNK
BINS = LOWBIN + np.concatenate([np.arange(0, F, 2), np.arange(1, F, 2)])
VMEM_LIMIT = 56 * 1024 * 1024


def moved(block, source_of):
    count = lax.axis_size("blk")
    return lax.ppermute(block, "blk", [(source_of(i) % count, i) for i in range(count)])


def inverse_table():
    bin_index = jnp.asarray(BINS, jnp.int32)[:, None]
    lag_index = jnp.arange(NLAG, dtype=jnp.int32)[None, :] - LAG + WS
    residue = (bin_index * lag_index % WS).astype(jnp.float32)
    angles = 2.0 * math.pi / WS * residue
    table = jnp.concatenate([jnp.cos(angles), -jnp.sin(angles)], axis=0)
    return table.astype(jnp.bfloat16)


def forward_table():
    angles = 2.0 * np.pi / WS * (BINS[:, None] * np.arange(HALF)[None, :] % WS)
    even, odd = angles[: F // 2], angles[F // 2 :]
    table = np.concatenate([np.cos(even), -np.sin(even), np.cos(odd), -np.sin(odd)])
    table = table.reshape(2 * F, STEPS, CHUNK).transpose(1, 0, 2)
    return np.ascontiguousarray(table).astype(np.float32).astype(jnp.bfloat16)


def spectrum_kernel(capacity, id_ref, x0_ref, x1_ref, table_ref, out_ref, first, second):
    step = pl.program_id(0)

    @pl.when(step == 0)
    def _():
        first[...] = jnp.dot(table_ref[...], x0_ref[...], preferred_element_type=jnp.float32)
        second[...] = jnp.dot(table_ref[...], x1_ref[...], preferred_element_type=jnp.float32)

    @pl.when(step > 0)
    def _():
        first[...] += jnp.dot(table_ref[...], x0_ref[...], preferred_element_type=jnp.float32)
        second[...] += jnp.dot(table_ref[...], x1_ref[...], preferred_element_type=jnp.float32)

    @pl.when(step == STEPS - 1)
    def _():
        rec_count = id_ref.shape[1]
        owner = id_ref[...] // rec_count
        row = jnp.broadcast_to(owner, (rec_count, rec_count))
        before = lax.broadcasted_iota(jnp.int32, row.shape, 0) < lax.broadcasted_iota(
            jnp.int32, row.shape, 1
        )
        rank = jnp.sum(jnp.where((row == row.T) & before, 1, 0), axis=0, keepdims=True)
        target = owner * capacity + rank
        slot = lax.broadcasted_iota(jnp.int32, (out_ref.shape[0], rec_count), 0)
        pick = jnp.where(slot == target, 1.0, 0.0).astype(jnp.bfloat16)
        first[:F, :] += second[:F, :]
        first[F:, :] -= second[F:, :]
        power = jnp.sum(first[...] * first[...], axis=0, keepdims=True) / F
        scale = lax.rsqrt(power + 1e-06)
        half = F // 2
        for place, base in enumerate((0, F, half, F + half)):
            white = (first[base : base + half, :] * scale).astype(jnp.bfloat16)
            out_ref[:, place * half : (place + 1) * half] = lax.dot_general(
                pick, white, (((1,), (1,)), ((), ())), preferred_element_type=jnp.float32
            ).astype(jnp.bfloat16)


def spectra(traces, record_id, capacity, slots):
    rec_count = traces.shape[0]
    lanes = traces.T
    return pl.pallas_call(
        functools.partial(spectrum_kernel, capacity),
        grid=(STEPS,),
        in_specs=[
            pl.BlockSpec((1, rec_count), lambda i: (0, 0)),
            pl.BlockSpec((CHUNK, rec_count), lambda i: (i, 0)),
            pl.BlockSpec((CHUNK, rec_count), lambda i: (i + STEPS, 0)),
            pl.BlockSpec((None, 2 * F, CHUNK), lambda i: (i, 0, 0)),
        ],
        out_specs=pl.BlockSpec((slots, 2 * F), lambda i: (0, 0)),
        out_shape=jax.ShapeDtypeStruct((slots, 2 * F), jnp.bfloat16),
        scratch_shapes=[
            pltpu.VMEM((2 * F, rec_count), jnp.float32),
            pltpu.VMEM((2 * F, rec_count), jnp.float32),
        ],
        compiler_params=pltpu.CompilerParams(vmem_limit_bytes=VMEM_LIMIT),
        cost_estimate=pl.CostEstimate(
            flops=4 * rec_count * WS * F, bytes_accessed=2 * WS * (rec_count + F), transcendentals=0
        ),
        name="spectra",
    )(record_id.reshape(1, rec_count), lanes, lanes, jnp.asarray(forward_table()))


def rows_kernel(capacity, me_ref, id_ref, row_ref):
    ids = id_ref[...]
    peers, rec_count = ids.shape
    hit = ids // rec_count == me_ref[0]
    before = lax.broadcasted_iota(jnp.int32, (rec_count, rec_count), 0) < lax.broadcasted_iota(
        jnp.int32, (rec_count, rec_count), 1
    )
    rank = jnp.dot(
        jnp.where(hit, 1.0, 0.0).astype(jnp.bfloat16),
        jnp.where(before, 1.0, 0.0).astype(jnp.bfloat16),
        preferred_element_type=jnp.float32,
    ).astype(jnp.int32)
    local = (ids % rec_count + 1).astype(jnp.float32)
    slots = row_ref.shape[1]
    slot = lax.broadcasted_iota(jnp.int32, (1, slots), 1)
    peer = lax.broadcasted_iota(jnp.int32, (peers, slots), 0)
    label = jnp.zeros((peers, slots), jnp.float32)
    for j in range(capacity):
        value = jnp.sum(jnp.where(hit & (rank == j), local, 0.0), axis=1, keepdims=True)
        label = jnp.where(slot == peer * capacity + j, value, label)
    label = jnp.sum(label, axis=0, keepdims=True).astype(jnp.int32) - 1
    row = label % NWIN * (rec_count // NWIN) + label // NWIN
    row_ref[...] = jnp.where(label >= 0, row, -1)


def arrival_rows(all_ids, capacity):
    peers = all_ids.shape[0]
    me = lax.axis_index("blk").astype(jnp.int32).reshape(1)
    return pl.pallas_call(
        functools.partial(rows_kernel, capacity),
        in_specs=[pl.BlockSpec(memory_space=pltpu.SMEM), pl.BlockSpec(memory_space=pltpu.VMEM)],
        out_shape=jax.ShapeDtypeStruct((1, peers * capacity), jnp.int32),
        name="rows",
    )(me, all_ids)


def place_kernel(row_ref, arrived_ref, out_ref):
    want = lax.broadcasted_iota(jnp.int32, (out_ref.shape[0], row_ref.shape[1]), 0)
    pick = jnp.where(want == row_ref[...], 1.0, 0.0).astype(jnp.bfloat16)
    out_ref[...] = jnp.dot(pick, arrived_ref[...], preferred_element_type=jnp.float32).astype(
        jnp.bfloat16
    )


def place(rows, arrived, rec_count):
    return pl.pallas_call(
        place_kernel,
        out_shape=jax.ShapeDtypeStruct((rec_count, 2 * F), jnp.bfloat16),
        compiler_params=pltpu.CompilerParams(vmem_limit_bytes=VMEM_LIMIT),
        name="place",
    )(rows, arrived)


def correlate_kernel(hop_index, group, *refs):
    own_ref, other_ref, inverse_ref = refs[1:4]
    out_ref, mine, theirs, cross = refs[-4:]
    width = own_ref.shape[0] // NWIN
    step = pl.program_id(0)

    @pl.when(step == 0)
    def _():
        for w in range(NWIN):
            rows = slice(w * width, (w + 1) * width)
            real = own_ref[rows, :F].astype(jnp.float32)
            imag = own_ref[rows, F:].astype(jnp.float32)
            mine[0, rows, :] = real + imag
            mine[1, rows, :] = real
            mine[2, rows, :] = imag
            real = other_ref[rows, :F].astype(jnp.float32)
            imag = other_ref[rows, F:].astype(jnp.float32)
            theirs[0, rows, :] = real
            theirs[1, rows, :] = real + imag
            theirs[2, rows, :] = real - imag

    blocks = [
        pl.ds(pl.multiple_of(w * width + step * group, group), group) for w in range(NWIN)
    ]
    for tile in range(F // 128):
        lanes = slice(tile * 128, (tile + 1) * 128)
        for first in range(0, group, 2):
            total = [[None] * 3 for _ in range(2)]
            for w in range(NWIN):
                for j in range(3):
                    factor = theirs[j, w * width : (w + 1) * width, lanes]
                    rows = mine.at[j, blocks[w], lanes]
                    for c in range(2):
                        term = factor * rows[first + c : first + c + 1, :]
                        total[c][j] = term if w == 0 else total[c][j] + term
            for c in range(2):
                rows = slice((first + c) * width, (first + c + 1) * width)
                cross[rows, tile * 128 : (tile + 1) * 128] = (total[c][0] - total[c][2]).astype(
                    jnp.bfloat16
                )
                cross[rows, F + tile * 128 : F + (tile + 1) * 128] = (
                    total[c][0] - total[c][1]
                ).astype(jnp.bfloat16)
    lagged = jnp.dot(cross[...], inverse_ref[...], preferred_element_type=jnp.float32)
    lagged = (lagged * (1.0 / math.sqrt(F * NWIN))).reshape(group, width, NLAG)
    if hop_index == 0:
        shape = (group, width, NLAG)
        channel = lax.broadcasted_iota(jnp.int32, shape, 0) + step * group
        lagged = jnp.where(channel == lax.broadcasted_iota(jnp.int32, shape, 1), 0.0, lagged)
    out_ref[...] = lagged.astype(jnp.bfloat16)[:, None]


def correlate(own, other, inverse, hop, result):
    rec_count = own.shape[0]
    width = rec_count // NWIN
    group = 8
    whole = lambda shape: pl.BlockSpec(shape, lambda i, h: (0,) * len(shape))
    in_specs = [whole(own.shape), whole(other.shape), whole(inverse.shape)]
    operands = [jnp.asarray(hop, jnp.int32).reshape(1), own, other, inverse]
    aliases = {}
    if result is not None:
        in_specs.append(pl.BlockSpec(memory_space=pl.ANY))
        operands.append(result)
        aliases = {4: 0}
    pairs = width * width
    return pl.pallas_call(
        functools.partial(correlate_kernel, hop if isinstance(hop, int) else None, group),
        grid_spec=pltpu.PrefetchScalarGridSpec(
            num_scalar_prefetch=1,
            grid=(width // group,),
            in_specs=in_specs,
            out_specs=pl.BlockSpec((group, 1, width, NLAG), lambda i, h: (i, h[0], 0, 0)),
            scratch_shapes=[
                pltpu.VMEM((3, rec_count, F), jnp.float32),
                pltpu.VMEM((3, rec_count, F), jnp.float32),
                pltpu.VMEM((group * width, 2 * F), jnp.bfloat16),
            ],
        ),
        out_shape=jax.ShapeDtypeStruct((width, HOPS + 1, width, NLAG), jnp.bfloat16),
        input_output_aliases=aliases,
        compiler_params=pltpu.CompilerParams(vmem_limit_bytes=VMEM_LIMIT),
        cost_estimate=pl.CostEstimate(
            flops=pairs * 2 * F * NLAG * 4, bytes_accessed=pairs * NLAG * 2, transcendentals=0
        ),
        name="correlate",
    )(*operands)


def on_device(traces, record_id):
    rec_count = traces.shape[0]
    peers = lax.axis_size("blk")
    capacity = 2 * rec_count // peers
    slots = peers * capacity
    all_ids = lax.all_to_all(
        jnp.broadcast_to(record_id[None, None], (peers, 1, rec_count)),
        "blk",
        split_axis=0,
        concat_axis=0,
        tiled=True,
    ).reshape(peers, rec_count)
    outgoing = spectra(traces, record_id, capacity, slots).reshape(peers, capacity, 2 * F)
    arrived = lax.all_to_all(outgoing, "blk", split_axis=0, concat_axis=0, tiled=True)
    arrived, rows, inverse = lax.optimization_barrier(
        (arrived, arrival_rows(all_ids, capacity), inverse_table())
    )
    own = place(rows, arrived.reshape(slots, 2 * F), rec_count)

    odd = lax.axis_index("blk") % 2
    near_hop, far_hop = 1 + 2 * odd, 3 - 2 * odd
    ahead = moved(own, lambda i: i + 2)
    near = moved(own, lambda i: i + 3 if i % 2 else i + 1)
    result = correlate(own, own, inverse, 0, None)
    ahead, result = lax.optimization_barrier((ahead, result))
    far = moved(ahead, lambda i: i ^ 1)
    result = correlate(own, ahead, inverse, 2, result)
    near, result = lax.optimization_barrier((near, result))
    result = correlate(own, near, inverse, near_hop, result)
    far, result = lax.optimization_barrier((far, result))
    return correlate(own, far, inverse, far_hop, result)


def solution(mesh):
    return jax.shard_map(
        on_device,
        mesh=mesh,
        in_specs=(P(("groups", "blk"), None), P(("groups", "blk"))),
        out_specs=P(("groups", "blk"), None, None, None),
        check_vma=False,
    )
```

```python
import functools
import math

import jax
import jax.numpy as jnp
import numpy as np
from jax import lax
from jax.experimental import pallas as pl
from jax.experimental.pallas import tpu as pltpu
from jax.sharding import PartitionSpec as P

NWIN = 8
WS = 12000
F = 512
LOWBIN = 60
LAG = 400
HOPS = 3
NLAG = 2 * LAG + 1
HALF = WS // 2
CHUNK = 1200
STEPS = HALF // CHUNK
PLUS = 384
LANES = 512
BINS = LOWBIN + np.concatenate([np.arange(0, F, 2), np.arange(1, F, 2)])
MIB = 1024 * 1024


def moved(block, source_of):
    count = lax.axis_size("blk")
    return lax.ppermute(block, "blk", [(source_of(i) % count, i) for i in range(count)])


def inverse_table():
    bin_index = jnp.asarray(BINS, jnp.int32)[:, None]
    lag_index = jnp.arange(LANES, dtype=jnp.int32)[None, :] - (LAG - PLUS) + WS
    residue = (bin_index * lag_index % WS).astype(jnp.float32)
    angles = 2.0 * math.pi / WS * residue
    return jnp.cos(angles).astype(jnp.bfloat16), (-jnp.sin(angles)).astype(jnp.bfloat16)


def forward_table():
    angles = 2.0 * np.pi / WS * (BINS[:, None] * np.arange(HALF)[None, :] % WS)
    even, odd = angles[: F // 2], angles[F // 2 :]
    table = np.concatenate([np.cos(even), -np.sin(even), np.cos(odd), -np.sin(odd)])
    table = table.reshape(2 * F, STEPS, CHUNK).transpose(1, 0, 2)
    return np.ascontiguousarray(table).astype(np.float32).astype(jnp.bfloat16)


def spectrum_kernel(capacity, id_ref, x0_ref, x1_ref, table_ref, out_ref, first, second):
    step = pl.program_id(0)

    @pl.when(step == 0)
    def _():
        first[...] = jnp.dot(table_ref[...], x0_ref[...], preferred_element_type=jnp.float32)
        second[...] = jnp.dot(table_ref[...], x1_ref[...], preferred_element_type=jnp.float32)

    @pl.when(step > 0)
    def _():
        first[...] += jnp.dot(table_ref[...], x0_ref[...], preferred_element_type=jnp.float32)
        second[...] += jnp.dot(table_ref[...], x1_ref[...], preferred_element_type=jnp.float32)

    @pl.when(step == STEPS - 1)
    def _():
        rec_count = id_ref.shape[1]
        owner = id_ref[...] // rec_count
        row = jnp.broadcast_to(owner, (rec_count, rec_count))
        before = lax.broadcasted_iota(jnp.int32, row.shape, 0) < lax.broadcasted_iota(
            jnp.int32, row.shape, 1
        )
        rank = jnp.sum(jnp.where((row == row.T) & before, 1, 0), axis=0, keepdims=True)
        target = owner * capacity + rank
        slot = lax.broadcasted_iota(jnp.int32, (out_ref.shape[0], rec_count), 0)
        pick = jnp.where(slot == target, 1.0, 0.0).astype(jnp.bfloat16)
        first[:F, :] += second[:F, :]
        first[F:, :] -= second[F:, :]
        power = jnp.sum(first[...] * first[...], axis=0, keepdims=True) / F
        scale = lax.rsqrt(power + 1e-06)
        half = F // 2
        for place, base in enumerate((0, F, half, F + half)):
            white = (first[base : base + half, :] * scale).astype(jnp.bfloat16)
            out_ref[:, place * half : (place + 1) * half] = lax.dot_general(
                pick, white, (((1,), (1,)), ((), ())), preferred_element_type=jnp.float32
            ).astype(jnp.bfloat16)


def spectra(traces, record_id, capacity, slots):
    rec_count = traces.shape[0]
    lanes = traces.T
    return pl.pallas_call(
        functools.partial(spectrum_kernel, capacity),
        grid=(STEPS,),
        in_specs=[
            pl.BlockSpec((1, rec_count), lambda i: (0, 0)),
            pl.BlockSpec((CHUNK, rec_count), lambda i: (i, 0)),
            pl.BlockSpec((CHUNK, rec_count), lambda i: (i + STEPS, 0)),
            pl.BlockSpec((None, 2 * F, CHUNK), lambda i: (i, 0, 0)),
        ],
        out_specs=pl.BlockSpec((slots, 2 * F), lambda i: (0, 0)),
        out_shape=jax.ShapeDtypeStruct((slots, 2 * F), jnp.bfloat16),
        scratch_shapes=[
            pltpu.VMEM((2 * F, rec_count), jnp.float32),
            pltpu.VMEM((2 * F, rec_count), jnp.float32),
        ],
        compiler_params=pltpu.CompilerParams(vmem_limit_bytes=56 * MIB),
        cost_estimate=pl.CostEstimate(
            flops=4 * rec_count * WS * F, bytes_accessed=2 * WS * (rec_count + F), transcendentals=0
        ),
        name="spectra",
    )(record_id.reshape(1, rec_count), lanes, lanes, jnp.asarray(forward_table()))


def rows_kernel(capacity, me_ref, id_ref, row_ref):
    ids = id_ref[...]
    peers, rec_count = ids.shape
    hit = ids // rec_count == me_ref[0]
    before = lax.broadcasted_iota(jnp.int32, (rec_count, rec_count), 0) < lax.broadcasted_iota(
        jnp.int32, (rec_count, rec_count), 1
    )
    rank = jnp.dot(
        jnp.where(hit, 1.0, 0.0).astype(jnp.bfloat16),
        jnp.where(before, 1.0, 0.0).astype(jnp.bfloat16),
        preferred_element_type=jnp.float32,
    ).astype(jnp.int32)
    local = (ids % rec_count + 1).astype(jnp.float32)
    slots = row_ref.shape[1]
    slot = lax.broadcasted_iota(jnp.int32, (1, slots), 1)
    peer = lax.broadcasted_iota(jnp.int32, (peers, slots), 0)
    label = jnp.zeros((peers, slots), jnp.float32)
    for j in range(capacity):
        value = jnp.sum(jnp.where(hit & (rank == j), local, 0.0), axis=1, keepdims=True)
        label = jnp.where(slot == peer * capacity + j, value, label)
    label = jnp.sum(label, axis=0, keepdims=True).astype(jnp.int32) - 1
    row = label % NWIN * (rec_count // NWIN) + label // NWIN
    row_ref[...] = jnp.where(label >= 0, row, -1)


def arrival_rows(all_ids, capacity):
    peers = all_ids.shape[0]
    me = lax.axis_index("blk").astype(jnp.int32).reshape(1)
    return pl.pallas_call(
        functools.partial(rows_kernel, capacity),
        in_specs=[pl.BlockSpec(memory_space=pltpu.SMEM), pl.BlockSpec(memory_space=pltpu.VMEM)],
        out_shape=jax.ShapeDtypeStruct((1, peers * capacity), jnp.int32),
        name="rows",
    )(me, all_ids)


def place_kernel(row_ref, arrived_ref, out_ref):
    want = lax.broadcasted_iota(jnp.int32, (out_ref.shape[0], row_ref.shape[1]), 0)
    pick = jnp.where(want == row_ref[...], 1.0, 0.0).astype(jnp.bfloat16)
    out_ref[...] = jnp.dot(pick, arrived_ref[...], preferred_element_type=jnp.float32).astype(
        jnp.bfloat16
    )


def place(rows, arrived, rec_count):
    return pl.pallas_call(
        place_kernel,
        out_shape=jax.ShapeDtypeStruct((rec_count, 2 * F), jnp.bfloat16),
        compiler_params=pltpu.CompilerParams(vmem_limit_bytes=8 * MIB),
        name="place",
    )(rows, arrived)


def correlate_kernel(hop_index, group, *refs):
    own_ref, other_ref, cos_ref, sin_ref = refs[1:5]
    out_ref, mine, theirs, cross = refs[-4:]
    width = own_ref.shape[0] // NWIN
    step = pl.program_id(0)

    @pl.when(step == 0)
    def _():
        for w in range(NWIN):
            rows = slice(w * width, (w + 1) * width)
            real = own_ref[rows, :F].astype(jnp.float32)
            imag = own_ref[rows, F:].astype(jnp.float32)
            mine[0, rows, :] = real + imag
            mine[1, rows, :] = real
            mine[2, rows, :] = imag
            real = other_ref[rows, :F].astype(jnp.float32)
            imag = other_ref[rows, F:].astype(jnp.float32)
            theirs[0, rows, :] = real
            theirs[1, rows, :] = real + imag
            theirs[2, rows, :] = real - imag

    blocks = [
        pl.ds(pl.multiple_of(w * width + step * group, group), group) for w in range(NWIN)
    ]
    for tile in range(F // 128):
        lanes = slice(tile * 128, (tile + 1) * 128)
        for first in range(0, group, 2):
            total = [[None] * 3 for _ in range(2)]
            for w in range(NWIN):
                for j in range(3):
                    factor = theirs[j, w * width : (w + 1) * width, lanes]
                    rows = mine.at[j, blocks[w], lanes]
                    for c in range(2):
                        term = factor * rows[first + c : first + c + 1, :]
                        total[c][j] = term if w == 0 else total[c][j] + term
            for c in range(2):
                rows = slice((first + c) * width, (first + c + 1) * width)
                cross[rows, tile * 128 : (tile + 1) * 128] = (total[c][0] - total[c][2]).astype(
                    jnp.bfloat16
                )
                cross[rows, F + tile * 128 : F + (tile + 1) * 128] = (
                    total[c][0] - total[c][1]
                ).astype(jnp.bfloat16)
    unit = 1.0 / math.sqrt(F * NWIN)
    even = jnp.dot(cross[:, :F], cos_ref[...], preferred_element_type=jnp.float32)
    uneven = jnp.dot(cross[:, F:], sin_ref[...], preferred_element_type=jnp.float32)
    later = (even + uneven) * unit
    earlier = (even - uneven) * unit
    rows = group * width
    lane = lax.broadcasted_iota(jnp.int32, (rows, 128), 1)
    last = (2 * LAG - PLUS) % 128
    mirror = (last - lane) & 127
    turned = [
        jnp.take_along_axis(earlier[:, q * 128 : (q + 1) * 128], mirror, axis=1)
        for q in range(LANES // 128)
    ]
    top = (2 * LAG - PLUS) // 128
    pieces = [jnp.where(lane <= last, turned[top - t], turned[top - 1 - t]) for t in range(PLUS // 128)]
    lagged = jnp.concatenate(pieces + [later[:, : NLAG - PLUS]], axis=1).reshape(group, width, NLAG)
    if hop_index == 0:
        shape = (group, width, NLAG)
        channel = lax.broadcasted_iota(jnp.int32, shape, 0) + step * group
        lagged = jnp.where(channel == lax.broadcasted_iota(jnp.int32, shape, 1), 0.0, lagged)
    out_ref[...] = lagged.astype(jnp.bfloat16)[:, None]


def correlate(own, other, inverse, hop, result):
    rec_count = own.shape[0]
    width = rec_count // NWIN
    group = 8
    whole = lambda shape: pl.BlockSpec(shape, lambda i, h: (0,) * len(shape))
    in_specs = [whole(own.shape), whole(other.shape), whole((F, LANES)), whole((F, LANES))]
    operands = [jnp.asarray(hop, jnp.int32).reshape(1), own, other, *inverse]
    aliases = {}
    if result is not None:
        in_specs.append(pl.BlockSpec(memory_space=pl.ANY))
        operands.append(result)
        aliases = {5: 0}
    pairs = width * width
    return pl.pallas_call(
        functools.partial(correlate_kernel, hop if isinstance(hop, int) else None, group),
        grid_spec=pltpu.PrefetchScalarGridSpec(
            num_scalar_prefetch=1,
            grid=(width // group,),
            in_specs=in_specs,
            out_specs=pl.BlockSpec((group, 1, width, NLAG), lambda i, h: (i, h[0], 0, 0)),
            scratch_shapes=[
                pltpu.VMEM((3, rec_count, F), jnp.float32),
                pltpu.VMEM((3, rec_count, F), jnp.float32),
                pltpu.VMEM((group * width, 2 * F), jnp.bfloat16),
            ],
        ),
        out_shape=jax.ShapeDtypeStruct((width, HOPS + 1, width, NLAG), jnp.bfloat16),
        input_output_aliases=aliases,
        compiler_params=pltpu.CompilerParams(vmem_limit_bytes=14 * MIB),
        cost_estimate=pl.CostEstimate(
            flops=pairs * 2 * F * NLAG * 4, bytes_accessed=pairs * NLAG * 2, transcendentals=0
        ),
        name="correlate",
    )(*operands)


def on_device(traces, record_id):
    rec_count = traces.shape[0]
    peers = lax.axis_size("blk")
    capacity = 2 * rec_count // peers
    slots = peers * capacity
    outgoing = spectra(traces, record_id, capacity, slots).reshape(peers, capacity, 2 * F)
    outgoing, ids = lax.optimization_barrier((outgoing, record_id))
    arrived = lax.all_to_all(outgoing, "blk", split_axis=0, concat_axis=0, tiled=True)
    all_ids = lax.all_to_all(
        jnp.broadcast_to(ids[None, None], (peers, 1, rec_count)),
        "blk",
        split_axis=0,
        concat_axis=0,
        tiled=True,
    ).reshape(peers, rec_count)
    arrived, rows, inverse = lax.optimization_barrier(
        (arrived, arrival_rows(all_ids, capacity), inverse_table())
    )
    own = place(rows, arrived.reshape(slots, 2 * F), rec_count)

    odd = lax.axis_index("blk") % 2
    near_hop, far_hop = 1 + 2 * odd, 3 - 2 * odd
    ahead = moved(own, lambda i: i + 2)
    near = moved(own, lambda i: i + 3 if i % 2 else i + 1)
    result = correlate(own, own, inverse, 0, None)
    ahead, result = lax.optimization_barrier((ahead, result))
    far = moved(ahead, lambda i: i ^ 1)
    result = correlate(own, ahead, inverse, 2, result)
    near, result = lax.optimization_barrier((near, result))
    result = correlate(own, near, inverse, near_hop, result)
    far, result = lax.optimization_barrier((far, result))
    return correlate(own, far, inverse, far_hop, result)


def solution(mesh):
    return jax.shard_map(
        on_device,
        mesh=mesh,
        in_specs=(P(("groups", "blk"), None), P(("groups", "blk"))),
        out_specs=P(("groups", "blk"), None, None, None),
        check_vma=False,
    )
```

```python
import functools
import math

import jax
import jax.numpy as jnp
import numpy as np
from jax import lax
from jax.experimental import pallas as pl
from jax.experimental.pallas import tpu as pltpu
from jax.sharding import PartitionSpec as P

NWIN = 8
WS = 12000
F = 512
LOWBIN = 60
LAG = 400
HOPS = 3
NLAG = 2 * LAG + 1
HALF = WS // 2
CHUNK = 1200
STEPS = HALF // CHUNK
PLUS = 384
LANES = 512
BINS = LOWBIN + np.concatenate([np.arange(0, F, 2), np.arange(1, F, 2)])
PACK = 4
TAIL = 128
MIB = 1024 * 1024


def moved(block, source_of):
    count = lax.axis_size("blk")
    return lax.ppermute(block, "blk", [(source_of(i) % count, i) for i in range(count)])


def inverse_table():
    bin_index = jnp.asarray(BINS, jnp.int32)[:, None]
    lag_index = jnp.arange(LANES, dtype=jnp.int32)[None, :] - (LAG - PLUS) + WS
    residue = (bin_index * lag_index % WS).astype(jnp.float32)
    angles = 2.0 * math.pi / WS * residue
    return jnp.cos(angles).astype(jnp.bfloat16), (-jnp.sin(angles)).astype(jnp.bfloat16)


def forward_table():
    angles = 2.0 * np.pi / WS * (BINS[:, None] * np.arange(HALF)[None, :] % WS)
    even, odd = angles[: F // 2], angles[F // 2 :]
    table = np.concatenate([np.cos(even), -np.sin(even), np.cos(odd), -np.sin(odd)])
    table = table.reshape(2 * F, STEPS, CHUNK).transpose(1, 0, 2)
    return np.ascontiguousarray(table).astype(np.float32).astype(jnp.bfloat16)


def spectrum_kernel(capacity, id_ref, x0_ref, x1_ref, table_ref, out_ref, even, odd):
    step = pl.program_id(0)

    def add(start):
        for part, total in enumerate((even, odd)):
            table = table_ref[part * F : (part + 1) * F, :]
            first = jnp.dot(table, x0_ref[...], preferred_element_type=jnp.float32)
            second = jnp.dot(table, x1_ref[...], preferred_element_type=jnp.float32)
            both = first + second if part == 0 else first - second
            total[...] = both if start else total[...] + both

    pl.when(step == 0)(functools.partial(add, True))
    pl.when(step > 0)(functools.partial(add, False))

    @pl.when(step == STEPS - 1)
    def _():
        rec_count = id_ref.shape[1]
        ids = id_ref[...]
        owner = ids // rec_count
        row = jnp.broadcast_to(owner, (rec_count, rec_count))
        before = lax.broadcasted_iota(jnp.int32, row.shape, 0) < lax.broadcasted_iota(
            jnp.int32, row.shape, 1
        )
        rank = jnp.sum(jnp.where((row == row.T) & before, 1, 0), axis=0, keepdims=True)
        target = owner * capacity + rank
        label = (ids % rec_count + 1).astype(jnp.float32)
        power = jnp.sum(even[...] * even[...], axis=0, keepdims=True)
        power = (power + jnp.sum(odd[...] * odd[...], axis=0, keepdims=True)) / F
        scale = lax.rsqrt(power + 1e-06)
        half = F // 2
        white = [
            (part[base : base + half, :] * scale).astype(jnp.bfloat16)
            for part, base in ((even, 0), (odd, 0), (even, half), (odd, half))
        ]
        rows = out_ref.shape[0]
        slot = lax.broadcasted_iota(jnp.int32, (rows, rec_count), 0) * PACK
        lane = lax.broadcasted_iota(jnp.int32, (rows, TAIL), 1)
        labels = jnp.zeros((rows, TAIL), jnp.float32)
        for q in range(PACK):
            hit = slot + q == target
            labels = jnp.where(
                lane == q, jnp.sum(jnp.where(hit, label, 0.0), axis=1, keepdims=True), labels
            )
            pick = jnp.where(hit, 1.0, 0.0).astype(jnp.bfloat16)
            for place, block in enumerate(white):
                base = q * 2 * F + place * half
                out_ref[:, base : base + half] = lax.dot_general(
                    pick, block, (((1,), (1,)), ((), ())), preferred_element_type=jnp.float32
                ).astype(jnp.bfloat16)
        out_ref[:, PACK * 2 * F :] = labels.astype(jnp.bfloat16)


def spectra(traces, record_id, capacity, slots):
    rec_count = traces.shape[0]
    lanes = traces.T
    shape = (slots // PACK, PACK * 2 * F + TAIL)
    return pl.pallas_call(
        functools.partial(spectrum_kernel, capacity),
        grid=(STEPS,),
        in_specs=[
            pl.BlockSpec((1, rec_count), lambda i: (0, 0)),
            pl.BlockSpec((CHUNK, rec_count), lambda i: (i, 0)),
            pl.BlockSpec((CHUNK, rec_count), lambda i: (i + STEPS, 0)),
            pl.BlockSpec((None, 2 * F, CHUNK), lambda i: (i, 0, 0)),
        ],
        out_specs=pl.BlockSpec(shape, lambda i: (0, 0)),
        out_shape=jax.ShapeDtypeStruct(shape, jnp.bfloat16),
        scratch_shapes=[
            pltpu.VMEM((F, rec_count), jnp.float32),
            pltpu.VMEM((F, rec_count), jnp.float32),
        ],
        compiler_params=pltpu.CompilerParams(vmem_limit_bytes=56 * MIB),
        cost_estimate=pl.CostEstimate(
            flops=4 * rec_count * WS * F, bytes_accessed=2 * WS * (rec_count + F), transcendentals=0
        ),
        name="spectra",
    )(record_id.reshape(1, rec_count), lanes, lanes, jnp.asarray(forward_table()))


def place_kernel(arrived_ref, out_ref):
    rec_count = out_ref.shape[0]
    rows = arrived_ref.shape[0]
    labels = arrived_ref[:, PACK * 2 * F :].astype(jnp.float32).T.astype(jnp.int32) - 1
    want = lax.broadcasted_iota(jnp.int32, (rec_count, rows), 0)
    total = None
    for q in range(PACK):
        label = labels[q : q + 1, :]
        row = jnp.where(label >= 0, label % NWIN * (rec_count // NWIN) + label // NWIN, -1)
        pick = jnp.where(want == row, 1.0, 0.0).astype(jnp.bfloat16)
        part = jnp.dot(
            pick,
            arrived_ref[:, q * 2 * F : (q + 1) * 2 * F],
            preferred_element_type=jnp.float32,
        )
        total = part if q == 0 else total + part
    out_ref[...] = total.astype(jnp.bfloat16)


def place(arrived, rec_count):
    return pl.pallas_call(
        place_kernel,
        out_shape=jax.ShapeDtypeStruct((rec_count, 2 * F), jnp.bfloat16),
        compiler_params=pltpu.CompilerParams(vmem_limit_bytes=8 * MIB),
        name="place",
    )(arrived)


def correlate_kernel(hop_index, group, *refs):
    own_ref, other_ref, cos_ref, sin_ref = refs[1:5]
    out_ref, mine, theirs, cross = refs[-4:]
    width = own_ref.shape[0] // NWIN
    step = pl.program_id(0)

    @pl.when(step == 0)
    def _():
        for w in range(NWIN):
            rows = slice(w * width, (w + 1) * width)
            real = own_ref[rows, :F].astype(jnp.float32)
            imag = own_ref[rows, F:].astype(jnp.float32)
            mine[0, rows, :] = real + imag
            mine[1, rows, :] = real
            mine[2, rows, :] = imag
            real = other_ref[rows, :F].astype(jnp.float32)
            imag = other_ref[rows, F:].astype(jnp.float32)
            theirs[0, rows, :] = real
            theirs[1, rows, :] = real + imag
            theirs[2, rows, :] = real - imag

    blocks = [
        pl.ds(pl.multiple_of(w * width + step * group, group), group) for w in range(NWIN)
    ]
    for tile in range(F // 128):
        lanes = slice(tile * 128, (tile + 1) * 128)
        for first in range(0, group, 2):
            total = [[None] * 3 for _ in range(2)]
            for w in range(NWIN):
                for j in range(3):
                    factor = theirs[j, w * width : (w + 1) * width, lanes]
                    rows = mine.at[j, blocks[w], lanes]
                    for c in range(2):
                        term = factor * rows[first + c : first + c + 1, :]
                        total[c][j] = term if w == 0 else total[c][j] + term
            for c in range(2):
                rows = slice((first + c) * width, (first + c + 1) * width)
                cross[rows, tile * 128 : (tile + 1) * 128] = (total[c][0] - total[c][2]).astype(
                    jnp.bfloat16
                )
                cross[rows, F + tile * 128 : F + (tile + 1) * 128] = (
                    total[c][0] - total[c][1]
                ).astype(jnp.bfloat16)
    unit = 1.0 / math.sqrt(F * NWIN)
    even = jnp.dot(cross[:, :F], cos_ref[...], preferred_element_type=jnp.float32)
    uneven = jnp.dot(cross[:, F:], sin_ref[...], preferred_element_type=jnp.float32)
    later = (even + uneven) * unit
    earlier = (even - uneven) * unit
    rows = group * width
    lane = lax.broadcasted_iota(jnp.int32, (rows, 128), 1)
    last = (2 * LAG - PLUS) % 128
    mirror = (last - lane) & 127
    turned = [
        jnp.take_along_axis(earlier[:, q * 128 : (q + 1) * 128], mirror, axis=1)
        for q in range(LANES // 128)
    ]
    top = (2 * LAG - PLUS) // 128
    pieces = [jnp.where(lane <= last, turned[top - t], turned[top - 1 - t]) for t in range(PLUS // 128)]
    lagged = jnp.concatenate(pieces + [later[:, : NLAG - PLUS]], axis=1).reshape(group, width, NLAG)
    if hop_index == 0:
        shape = (group, width, NLAG)
        channel = lax.broadcasted_iota(jnp.int32, shape, 0) + step * group
        lagged = jnp.where(channel == lax.broadcasted_iota(jnp.int32, shape, 1), 0.0, lagged)
    out_ref[...] = lagged.astype(jnp.bfloat16)[:, None]


def correlate(own, other, inverse, hop, result):
    rec_count = own.shape[0]
    width = rec_count // NWIN
    group = 8
    whole = lambda shape: pl.BlockSpec(shape, lambda i, h: (0,) * len(shape))
    in_specs = [whole(own.shape), whole(other.shape), whole((F, LANES)), whole((F, LANES))]
    operands = [jnp.asarray(hop, jnp.int32).reshape(1), own, other, *inverse]
    aliases = {}
    if result is not None:
        in_specs.append(pl.BlockSpec(memory_space=pl.ANY))
        operands.append(result)
        aliases = {5: 0}
    pairs = width * width
    return pl.pallas_call(
        functools.partial(correlate_kernel, hop if isinstance(hop, int) else None, group),
        grid_spec=pltpu.PrefetchScalarGridSpec(
            num_scalar_prefetch=1,
            grid=(width // group,),
            in_specs=in_specs,
            out_specs=pl.BlockSpec((group, 1, width, NLAG), lambda i, h: (i, h[0], 0, 0)),
            scratch_shapes=[
                pltpu.VMEM((3, rec_count, F), jnp.float32),
                pltpu.VMEM((3, rec_count, F), jnp.float32),
                pltpu.VMEM((group * width, 2 * F), jnp.bfloat16),
            ],
        ),
        out_shape=jax.ShapeDtypeStruct((width, HOPS + 1, width, NLAG), jnp.bfloat16),
        input_output_aliases=aliases,
        compiler_params=pltpu.CompilerParams(vmem_limit_bytes=14 * MIB),
        cost_estimate=pl.CostEstimate(
            flops=pairs * 2 * F * NLAG * 4, bytes_accessed=pairs * NLAG * 2, transcendentals=0
        ),
        name="correlate",
    )(*operands)


def on_device(traces, record_id):
    rec_count = traces.shape[0]
    peers = lax.axis_size("blk")
    capacity = 2 * rec_count // peers
    slots = peers * capacity
    outgoing = spectra(traces, record_id, capacity, slots)
    width = outgoing.shape[1]
    arrived = lax.all_to_all(
        outgoing.reshape(peers, capacity // PACK, width), "blk", split_axis=0, concat_axis=0, tiled=True
    )
    arrived, inverse = lax.optimization_barrier((arrived, inverse_table()))
    own = place(arrived.reshape(slots // PACK, width), rec_count)

    odd = lax.axis_index("blk") % 2
    near_hop, far_hop = 1 + 2 * odd, 3 - 2 * odd
    ahead = moved(own, lambda i: i + 2)
    near = moved(own, lambda i: i + 3 if i % 2 else i + 1)
    result = correlate(own, own, inverse, 0, None)
    ahead, result = lax.optimization_barrier((ahead, result))
    far = moved(ahead, lambda i: i ^ 1)
    result = correlate(own, ahead, inverse, 2, result)
    near, result = lax.optimization_barrier((near, result))
    result = correlate(own, near, inverse, near_hop, result)
    far, result = lax.optimization_barrier((far, result))
    return correlate(own, far, inverse, far_hop, result)


def solution(mesh):
    return jax.shard_map(
        on_device,
        mesh=mesh,
        in_specs=(P(("groups", "blk"), None), P(("groups", "blk"))),
        out_specs=P(("groups", "blk"), None, None, None),
        check_vma=False,
    )
```

```python
import functools
import math

import jax
import jax.numpy as jnp
import numpy as np
from jax import lax
from jax.experimental import pallas as pl
from jax.experimental.pallas import tpu as pltpu
from jax.sharding import PartitionSpec as P

NWIN = 8
WS = 12000
F = 512
LOWBIN = 60
LAG = 400
HOPS = 3
NLAG = 2 * LAG + 1
QUARTER = WS // 4
ENDS = (512, 1536, QUARTER)
PADDED = -(-QUARTER // 128) * 128
PLUS = 384
LANES = 512
FOURTH = F // 4
BINS = np.concatenate([LOWBIN + np.arange((m - LOWBIN) % 4, F, 4) for m in (0, 2, 1, 3)])
PACK = 4
TAIL = 128
MIB = 1024 * 1024


def moved(block, source_of):
    count = lax.axis_size("blk")
    return lax.ppermute(block, "blk", [(source_of(i) % count, i) for i in range(count)])


def inverse_table():
    bin_index = jnp.asarray(BINS, jnp.int32)[:, None]
    lag_index = jnp.arange(LANES, dtype=jnp.int32)[None, :] - (LAG - PLUS) + WS
    residue = (bin_index * lag_index % WS).astype(jnp.float32)
    angles = 2.0 * math.pi / WS * residue
    return jnp.cos(angles).astype(jnp.bfloat16), (-jnp.sin(angles)).astype(jnp.bfloat16)


def forward_table():
    angles = 2.0 * np.pi / WS * (BINS[:, None] * np.arange(QUARTER)[None, :] % WS)
    even, odd = np.split(angles, 2)
    table = np.zeros((2 * F, PADDED), np.float32)
    table[:, :QUARTER] = np.concatenate([np.cos(even), -np.sin(even), np.cos(odd), -np.sin(odd)])
    return table.astype(jnp.bfloat16)


def spectrum_kernel(capacity, id_ref, x_ref, table_ref, out_ref, samples, table, even, odd, sems):
    begins = (0,) + ENDS[:-1]
    copies = []
    for c, (begin, end) in enumerate(zip(begins, ENDS)):
        lanes = slice(begin, end if end < QUARTER else PADDED)
        pairs = [(table_ref.at[:, lanes], table.at[:, lanes])]
        for j in range(4):
            source = x_ref.at[j * QUARTER + begin : j * QUARTER + end, :]
            pairs.append((source, samples.at[j, begin:end, :]))
        copies.append(
            [pltpu.make_async_copy(a, b, sems.at[c, i]) for i, (a, b) in enumerate(pairs)]
        )
    for group in copies:
        for copy in group:
            copy.start()
    for group, begin, end in zip(copies, begins, ENDS):
        for copy in group:
            copy.wait()
        for turn, total in enumerate((even, odd)):
            rows = slice(turn * F, (turn + 1) * F)
            parts = [
                jnp.dot(
                    table[rows, begin:end],
                    samples[j, begin:end, :],
                    preferred_element_type=jnp.float32,
                )
                for j in range(4)
            ]
            if turn == 0:
                straight, across = parts[0] + parts[2], parts[1] + parts[3]
                signs, order = (1, -1, 1, -1), (0, 1, 2, 3)
            else:
                straight, across = parts[0] - parts[2], parts[1] - parts[3]
                signs, order = (1, -1, -1, 1), (2, 3, 0, 1)
            for block in range(4):
                mine = slice(block * FOURTH, (block + 1) * FOURTH)
                theirs = slice(order[block] * FOURTH, (order[block] + 1) * FOURTH)
                both = straight[mine] + across[theirs] if signs[block] > 0 else straight[mine] - across[theirs]
                total[mine, :] = both if begin == 0 else total[mine, :] + both

    rec_count = id_ref.shape[1]
    ids = id_ref[...]
    owner = ids // rec_count
    row = jnp.broadcast_to(owner, (rec_count, rec_count))
    before = lax.broadcasted_iota(jnp.int32, row.shape, 0) < lax.broadcasted_iota(
        jnp.int32, row.shape, 1
    )
    rank = jnp.sum(jnp.where((row == row.T) & before, 1, 0), axis=0, keepdims=True)
    target = owner * capacity + rank
    label = (ids % rec_count + 1).astype(jnp.float32)
    power = jnp.sum(even[...] * even[...], axis=0, keepdims=True)
    power = (power + jnp.sum(odd[...] * odd[...], axis=0, keepdims=True)) / F
    scale = lax.rsqrt(power + 1e-06)
    half = F // 2
    rows = out_ref.shape[0]
    slot = lax.broadcasted_iota(jnp.int32, (rows, rec_count), 0) * PACK
    lane = lax.broadcasted_iota(jnp.int32, (rows, TAIL), 1)
    labels = jnp.zeros((rows, TAIL), jnp.float32)
    picks = []
    for q in range(PACK):
        hit = slot + q == target
        labels = jnp.where(
            lane == q, jnp.sum(jnp.where(hit, label, 0.0), axis=1, keepdims=True), labels
        )
        picks.append(jnp.where(hit, 1.0, 0.0).astype(jnp.bfloat16))
    pick = jnp.concatenate(picks)
    for place, (part, base) in enumerate(((even, 0), (odd, 0), (even, half), (odd, half))):
        white = (part[base : base + half, :] * scale).astype(jnp.bfloat16)
        moved = lax.dot_general(
            pick, white, (((1,), (1,)), ((), ())), preferred_element_type=jnp.float32
        ).astype(jnp.bfloat16)
        for q in range(PACK):
            lanes = slice(q * 2 * F + place * half, q * 2 * F + (place + 1) * half)
            out_ref[:, lanes] = moved[q * rows : (q + 1) * rows]
    out_ref[:, PACK * 2 * F :] = labels.astype(jnp.bfloat16)


def spectra(traces, record_id, capacity, slots):
    rec_count = traces.shape[0]
    shape = (slots // PACK, PACK * 2 * F + TAIL)
    return pl.pallas_call(
        functools.partial(spectrum_kernel, capacity),
        in_specs=[
            pl.BlockSpec(memory_space=pltpu.VMEM),
            pl.BlockSpec(memory_space=pl.ANY),
            pl.BlockSpec(memory_space=pl.ANY),
        ],
        out_specs=pl.BlockSpec(memory_space=pltpu.VMEM),
        out_shape=jax.ShapeDtypeStruct(shape, jnp.bfloat16),
        scratch_shapes=[
            pltpu.VMEM((4, QUARTER, rec_count), jnp.bfloat16),
            pltpu.VMEM((2 * F, PADDED), jnp.bfloat16),
            pltpu.VMEM((F, rec_count), jnp.float32),
            pltpu.VMEM((F, rec_count), jnp.float32),
            pltpu.SemaphoreType.DMA((len(ENDS), 5)),
        ],
        compiler_params=pltpu.CompilerParams(vmem_limit_bytes=56 * MIB),
        cost_estimate=pl.CostEstimate(
            flops=4 * rec_count * WS * F, bytes_accessed=2 * WS * (rec_count + F), transcendentals=0
        ),
        name="spectra",
    )(record_id.reshape(1, rec_count), traces.T, jnp.asarray(forward_table()))


def place_kernel(arrived_ref, out_ref):
    rec_count = out_ref.shape[0]
    rows = arrived_ref.shape[0]
    labels = arrived_ref[:, PACK * 2 * F :].astype(jnp.float32).T.astype(jnp.int32) - 1
    want = lax.broadcasted_iota(jnp.int32, (rec_count, rows), 0)
    total = None
    for q in range(PACK):
        label = labels[q : q + 1, :]
        row = jnp.where(label >= 0, label % NWIN * (rec_count // NWIN) + label // NWIN, -1)
        pick = jnp.where(want == row, 1.0, 0.0).astype(jnp.bfloat16)
        part = jnp.dot(
            pick,
            arrived_ref[:, q * 2 * F : (q + 1) * 2 * F],
            preferred_element_type=jnp.float32,
        )
        total = part if q == 0 else total + part
    out_ref[...] = total.astype(jnp.bfloat16)


def place(arrived, rec_count):
    return pl.pallas_call(
        place_kernel,
        out_shape=jax.ShapeDtypeStruct((rec_count, 2 * F), jnp.bfloat16),
        compiler_params=pltpu.CompilerParams(vmem_limit_bytes=8 * MIB),
        name="place",
    )(arrived)


def correlate_kernel(hop_index, group, batch, *refs):
    hop_ref, own_ref, other_ref, cos_ref, sin_ref = refs[:5]
    out_ref, mine, theirs, cross, done, sems = refs[-6:]
    width = own_ref.shape[0] // NWIN
    for w in range(NWIN):
        rows = slice(w * width, (w + 1) * width)
        real = own_ref[rows, :F].astype(jnp.float32)
        imag = own_ref[rows, F:].astype(jnp.float32)
        mine[0, rows, :] = real + imag
        mine[1, rows, :] = real
        mine[2, rows, :] = imag
        real = other_ref[rows, :F].astype(jnp.float32)
        imag = other_ref[rows, F:].astype(jnp.float32)
        theirs[0, rows, :] = real
        theirs[1, rows, :] = real + imag
        theirs[2, rows, :] = real - imag

    def channels_from(step, carry):
        blocks = [
            pl.ds(pl.multiple_of(w * width + step * group, group), group) for w in range(NWIN)
        ]
        for tile in range(F // 128):
            lanes = slice(tile * 128, (tile + 1) * 128)
            for first in range(0, group, 2):
                total = [[None] * 3 for _ in range(2)]
                for w in range(NWIN):
                    for j in range(3):
                        factor = theirs[j, w * width : (w + 1) * width, lanes]
                        rows = mine.at[j, blocks[w], lanes]
                        for c in range(2):
                            term = factor * rows[first + c : first + c + 1, :]
                            total[c][j] = term if w == 0 else total[c][j] + term
                for c in range(2):
                    rows = pl.ds(
                        pl.multiple_of((step * group + first + c) * width, width), width
                    )
                    cross[rows, tile * 128 : (tile + 1) * 128] = (
                        total[c][0] - total[c][2]
                    ).astype(jnp.bfloat16)
                    cross[rows, F + tile * 128 : F + (tile + 1) * 128] = (
                        total[c][0] - total[c][1]
                    ).astype(jnp.bfloat16)
        return carry

    lax.fori_loop(0, width // group, channels_from, 0)
    unit = 1.0 / math.sqrt(F * NWIN)
    copies = []
    for step in range(width // batch):
        mine_rows = slice(step * batch * width, (step + 1) * batch * width)
        even = jnp.dot(cross[mine_rows, :F], cos_ref[...], preferred_element_type=jnp.float32)
        uneven = jnp.dot(cross[mine_rows, F:], sin_ref[...], preferred_element_type=jnp.float32)
        later = (even + uneven) * unit
        earlier = (even - uneven) * unit
        lane = lax.broadcasted_iota(jnp.int32, (batch * width, 128), 1)
        last = (2 * LAG - PLUS) % 128
        mirror = (last - lane) & 127
        turned = [
            jnp.take_along_axis(earlier[:, q * 128 : (q + 1) * 128], mirror, axis=1)
            for q in range(LANES // 128)
        ]
        top = (2 * LAG - PLUS) // 128
        pieces = [
            jnp.where(lane <= last, turned[top - t], turned[top - 1 - t]) for t in range(PLUS // 128)
        ]
        lagged = jnp.concatenate(pieces + [later[:, : NLAG - PLUS]], axis=1)
        lagged = lagged.reshape(batch, width, NLAG)
        if hop_index == 0:
            channel = lax.broadcasted_iota(jnp.int32, lagged.shape, 0) + step * batch
            partner = lax.broadcasted_iota(jnp.int32, lagged.shape, 1)
            lagged = jnp.where(channel == partner, 0.0, lagged)
        channels = slice(step * batch, (step + 1) * batch)
        done[channels] = lagged.astype(jnp.bfloat16)
        copy = pltpu.make_async_copy(
            done.at[channels], out_ref.at[channels, hop_ref[0]], sems.at[step]
        )
        copy.start()
        copies.append(copy)
    for copy in copies:
        copy.wait()


def correlate(own, other, inverse, hop, result):
    rec_count = own.shape[0]
    width = rec_count // NWIN
    group, batch = 8, 8
    operands = [jnp.asarray(hop, jnp.int32).reshape(1), own, other, *inverse]
    in_specs = [pl.BlockSpec(memory_space=pltpu.SMEM)]
    in_specs += [pl.BlockSpec(memory_space=pltpu.VMEM)] * 4
    aliases = {}
    if result is not None:
        in_specs.append(pl.BlockSpec(memory_space=pl.ANY))
        operands.append(result)
        aliases = {5: 0}
    pairs = width * width
    return pl.pallas_call(
        functools.partial(correlate_kernel, hop if isinstance(hop, int) else None, group, batch),
        in_specs=in_specs,
        out_specs=pl.BlockSpec(memory_space=pl.ANY),
        out_shape=jax.ShapeDtypeStruct((width, HOPS + 1, width, NLAG), jnp.bfloat16),
        scratch_shapes=[
            pltpu.VMEM((3, rec_count, F), jnp.float32),
            pltpu.VMEM((3, rec_count, F), jnp.float32),
            pltpu.VMEM((width * width, 2 * F), jnp.bfloat16),
            pltpu.VMEM((width, width, NLAG), jnp.bfloat16),
            pltpu.SemaphoreType.DMA((width // batch,)),
        ],
        input_output_aliases=aliases,
        compiler_params=pltpu.CompilerParams(vmem_limit_bytes=24 * MIB),
        cost_estimate=pl.CostEstimate(
            flops=pairs * 2 * F * NLAG * 4, bytes_accessed=pairs * NLAG * 2, transcendentals=0
        ),
        name="correlate",
    )(*operands)


def on_device(traces, record_id):
    rec_count = traces.shape[0]
    peers = lax.axis_size("blk")
    capacity = 2 * rec_count // peers
    slots = peers * capacity
    outgoing = spectra(traces, record_id, capacity, slots)
    width = outgoing.shape[1]
    arrived = lax.all_to_all(
        outgoing.reshape(peers, capacity // PACK, width), "blk", split_axis=0, concat_axis=0, tiled=True
    )
    arrived, inverse = lax.optimization_barrier((arrived, inverse_table()))
    own = place(arrived.reshape(slots // PACK, width), rec_count)

    odd = lax.axis_index("blk") % 2
    near_hop, far_hop = 1 + 2 * odd, 3 - 2 * odd
    ahead = moved(own, lambda i: i + 2)
    result = correlate(own, own, inverse, 0, None)
    own_again, result = lax.optimization_barrier((own, result))
    near = moved(own_again, lambda i: i + 3 if i % 2 else i + 1)
    ahead, result = lax.optimization_barrier((ahead, result))
    far = moved(ahead, lambda i: i ^ 1)
    result = correlate(own, ahead, inverse, 2, result)
    near, result = lax.optimization_barrier((near, result))
    result = correlate(own, near, inverse, near_hop, result)
    far, result = lax.optimization_barrier((far, result))
    return correlate(own, far, inverse, far_hop, result)


def solution(mesh):
    return jax.shard_map(
        on_device,
        mesh=mesh,
        in_specs=(P(("groups", "blk"), None), P(("groups", "blk"))),
        out_specs=P(("groups", "blk"), None, None, None),
        check_vma=False,
    )
```

```python
import functools
import math

import jax
import jax.numpy as jnp
import numpy as np
from jax import lax
from jax.experimental import pallas as pl
from jax.experimental.pallas import tpu as pltpu
from jax.sharding import PartitionSpec as P

NWIN = 8
WS = 12000
F = 512
LOWBIN = 60
LAG = 400
HOPS = 3
NLAG = 2 * LAG + 1
QUARTER = WS // 4
ENDS = (512, 1536, QUARTER)
PADDED = -(-QUARTER // 128) * 128
PLUS = 384
LANES = 512
FOURTH = F // 4
BINS = np.concatenate([LOWBIN + np.arange((m - LOWBIN) % 4, F, 4) for m in (0, 2, 1, 3)])
PACK = 4
TAIL = 128
MIB = 1024 * 1024


def moved(block, source_of):
    count = lax.axis_size("blk")
    return lax.ppermute(block, "blk", [(source_of(i) % count, i) for i in range(count)])


def inverse_table():
    bin_index = jnp.asarray(BINS, jnp.int32)[:, None]
    lag_index = jnp.arange(LANES, dtype=jnp.int32)[None, :] - (LAG - PLUS) + WS
    residue = (bin_index * lag_index % WS).astype(jnp.float32)
    angles = 2.0 * math.pi / WS * residue
    return jnp.cos(angles).astype(jnp.bfloat16), (-jnp.sin(angles)).astype(jnp.bfloat16)


def forward_table():
    angles = 2.0 * np.pi / WS * (BINS[:, None] * np.arange(QUARTER)[None, :] % WS)
    even, odd = np.split(angles, 2)
    table = np.zeros((2 * F, PADDED), np.float32)
    table[:, :QUARTER] = np.concatenate([np.cos(even), -np.sin(even), np.cos(odd), -np.sin(odd)])
    return table.astype(jnp.bfloat16)


def spectrum_kernel(capacity, id_ref, x_ref, table_ref, out_ref, samples, table, even, odd, sems):
    begins = (0,) + ENDS[:-1]
    copies = []
    for c, (begin, end) in enumerate(zip(begins, ENDS)):
        lanes = slice(begin, end if end < QUARTER else PADDED)
        pairs = [(table_ref.at[:, lanes], table.at[:, lanes])]
        for j in range(4):
            source = x_ref.at[j * QUARTER + begin : j * QUARTER + end, :]
            pairs.append((source, samples.at[j, begin:end, :]))
        copies.append(
            [pltpu.make_async_copy(a, b, sems.at[c, i]) for i, (a, b) in enumerate(pairs)]
        )
    for group in copies:
        for copy in group:
            copy.start()
    for group, begin, end in zip(copies, begins, ENDS):
        for copy in group:
            copy.wait()
        for turn, total in enumerate((even, odd)):
            rows = slice(turn * F, (turn + 1) * F)
            parts = [
                jnp.dot(
                    table[rows, begin:end],
                    samples[j, begin:end, :],
                    preferred_element_type=jnp.float32,
                )
                for j in range(4)
            ]
            if turn == 0:
                straight, across = parts[0] + parts[2], parts[1] + parts[3]
                signs, order = (1, -1, 1, -1), (0, 1, 2, 3)
            else:
                straight, across = parts[0] - parts[2], parts[1] - parts[3]
                signs, order = (1, -1, -1, 1), (2, 3, 0, 1)
            for block in range(4):
                mine = slice(block * FOURTH, (block + 1) * FOURTH)
                theirs = slice(order[block] * FOURTH, (order[block] + 1) * FOURTH)
                both = straight[mine] + across[theirs] if signs[block] > 0 else straight[mine] - across[theirs]
                total[mine, :] = both if begin == 0 else total[mine, :] + both

    rec_count = id_ref.shape[1]
    ids = id_ref[...]
    owner = ids // rec_count
    row = jnp.broadcast_to(owner, (rec_count, rec_count))
    before = lax.broadcasted_iota(jnp.int32, row.shape, 0) < lax.broadcasted_iota(
        jnp.int32, row.shape, 1
    )
    rank = jnp.sum(jnp.where((row == row.T) & before, 1, 0), axis=0, keepdims=True)
    target = owner * capacity + rank
    label = (ids % rec_count + 1).astype(jnp.float32)
    power = jnp.sum(even[...] * even[...], axis=0, keepdims=True)
    power = (power + jnp.sum(odd[...] * odd[...], axis=0, keepdims=True)) / F
    scale = lax.rsqrt(power + 1e-06)
    half = F // 2
    rows = out_ref.shape[0]
    slot = lax.broadcasted_iota(jnp.int32, (rows, rec_count), 0) * PACK
    lane = lax.broadcasted_iota(jnp.int32, (rows, TAIL), 1)
    labels = jnp.zeros((rows, TAIL), jnp.float32)
    picks = []
    for q in range(PACK):
        hit = slot + q == target
        labels = jnp.where(
            lane == q, jnp.sum(jnp.where(hit, label, 0.0), axis=1, keepdims=True), labels
        )
        picks.append(jnp.where(hit, 1.0, 0.0).astype(jnp.bfloat16))
    pick = jnp.concatenate(picks)
    for place, (part, base) in enumerate(((even, 0), (odd, 0), (even, half), (odd, half))):
        white = (part[base : base + half, :] * scale).astype(jnp.bfloat16)
        moved = lax.dot_general(
            pick, white, (((1,), (1,)), ((), ())), preferred_element_type=jnp.float32
        ).astype(jnp.bfloat16)
        for q in range(PACK):
            lanes = slice(q * 2 * F + place * half, q * 2 * F + (place + 1) * half)
            out_ref[:, lanes] = moved[q * rows : (q + 1) * rows]
    out_ref[:, PACK * 2 * F :] = labels.astype(jnp.bfloat16)


def spectra(traces, record_id, capacity, slots):
    rec_count = traces.shape[0]
    shape = (slots // PACK, PACK * 2 * F + TAIL)
    return pl.pallas_call(
        functools.partial(spectrum_kernel, capacity),
        in_specs=[
            pl.BlockSpec(memory_space=pltpu.VMEM),
            pl.BlockSpec(memory_space=pl.ANY),
            pl.BlockSpec(memory_space=pl.ANY),
        ],
        out_specs=pl.BlockSpec(memory_space=pltpu.VMEM),
        out_shape=jax.ShapeDtypeStruct(shape, jnp.bfloat16),
        scratch_shapes=[
            pltpu.VMEM((4, QUARTER, rec_count), jnp.bfloat16),
            pltpu.VMEM((2 * F, PADDED), jnp.bfloat16),
            pltpu.VMEM((F, rec_count), jnp.float32),
            pltpu.VMEM((F, rec_count), jnp.float32),
            pltpu.SemaphoreType.DMA((len(ENDS), 5)),
        ],
        compiler_params=pltpu.CompilerParams(vmem_limit_bytes=56 * MIB),
        cost_estimate=pl.CostEstimate(
            flops=4 * rec_count * WS * F, bytes_accessed=2 * WS * (rec_count + F), transcendentals=0
        ),
        name="spectra",
    )(record_id.reshape(1, rec_count), traces.T, jnp.asarray(forward_table()))


def place_kernel(arrived_ref, out_ref, *half_refs):
    rec_count = out_ref.shape[0]
    rows = arrived_ref.shape[0]
    side = rec_count // NWIN // 2
    labels = arrived_ref[:, PACK * 2 * F :].astype(jnp.float32).T.astype(jnp.int32) - 1
    want = lax.broadcasted_iota(jnp.int32, (rec_count, rows), 0)
    total = None
    for q in range(PACK):
        label = labels[q : q + 1, :]
        channel, window = label // NWIN, label % NWIN
        row = (channel // side * NWIN + window) * side + channel % side
        pick = jnp.where(want == jnp.where(label >= 0, row, -1), 1.0, 0.0).astype(jnp.bfloat16)
        part = jnp.dot(
            pick,
            arrived_ref[:, q * 2 * F : (q + 1) * 2 * F],
            preferred_element_type=jnp.float32,
        )
        total = part if q == 0 else total + part
    panel = total.astype(jnp.bfloat16)
    out_ref[...] = panel
    for half, ref in enumerate(half_refs):
        ref[...] = panel[half * rec_count // 2 : (half + 1) * rec_count // 2]


def place(arrived, rec_count):
    return pl.pallas_call(
        place_kernel,
        out_shape=[
            jax.ShapeDtypeStruct((rows, 2 * F), jnp.bfloat16)
            for rows in (rec_count, rec_count // 2, rec_count // 2)
        ],
        compiler_params=pltpu.CompilerParams(vmem_limit_bytes=8 * MIB),
        name="place",
    )(arrived)


def correlate_kernel(hop_index, begin, group, batch, count, *refs):
    hop_ref, own_ref = refs[:2]
    other_refs = refs[2 : 2 + count]
    cos_ref, sin_ref = refs[2 + count : 4 + count]
    out_ref, mine, theirs, cross, done, sems = refs[-6:]
    full = own_ref.shape[0] // NWIN
    side = full // 2
    width = theirs.shape[1] // NWIN
    own_blocks = [(own_ref, half * NWIN * side, half * side) for half in range(2)]
    if other_refs[0].shape[0] == own_ref.shape[0]:
        blocks = [(other_refs[0], half * NWIN * side, half * side) for half in range(2)]
    else:
        blocks = [(ref, 0, half * side) for half, ref in enumerate(other_refs)]
    for w in range(NWIN):
        for ref, base, place in own_blocks:
            source = slice(base + w * side, base + (w + 1) * side)
            rows = slice(w * full + place, w * full + place + side)
            real = ref[source, :F].astype(jnp.float32)
            imag = ref[source, F:].astype(jnp.float32)
            mine[0, rows, :] = real + imag
            mine[1, rows, :] = real
            mine[2, rows, :] = imag
        for ref, base, place in blocks:
            source = slice(base + w * side, base + (w + 1) * side)
            rows = slice(w * width + place, w * width + place + side)
            real = ref[source, :F].astype(jnp.float32)
            imag = ref[source, F:].astype(jnp.float32)
            theirs[0, rows, :] = real
            theirs[1, rows, :] = real + imag
            theirs[2, rows, :] = real - imag

    shared = 64 // width

    def channels_from(step, carry):
        blocks = [
            pl.ds(pl.multiple_of(w * full + step * group, group), group) for w in range(NWIN)
        ]
        for tile in range(F // 128):
            lanes = slice(tile * 128, (tile + 1) * 128)
            for first in range(0, group, shared):
                total = [[None] * 3 for _ in range(shared)]
                for w in range(NWIN):
                    for j in range(3):
                        factor = theirs[j, w * width : (w + 1) * width, lanes]
                        rows = mine.at[j, blocks[w], lanes]
                        for c in range(shared):
                            term = factor * rows[first + c : first + c + 1, :]
                            total[c][j] = term if w == 0 else total[c][j] + term
                for c in range(shared):
                    rows = pl.ds(
                        pl.multiple_of((step * group + first + c) * width, width), width
                    )
                    cross[rows, tile * 128 : (tile + 1) * 128] = (
                        total[c][0] - total[c][2]
                    ).astype(jnp.bfloat16)
                    cross[rows, F + tile * 128 : F + (tile + 1) * 128] = (
                        total[c][0] - total[c][1]
                    ).astype(jnp.bfloat16)
        return carry

    lax.fori_loop(0, full // group, channels_from, 0)
    unit = 1.0 / math.sqrt(F * NWIN)
    copies = []
    for step in range(full // batch):
        mine_rows = slice(step * batch * width, (step + 1) * batch * width)
        even = jnp.dot(cross[mine_rows, :F], cos_ref[...], preferred_element_type=jnp.float32)
        uneven = jnp.dot(cross[mine_rows, F:], sin_ref[...], preferred_element_type=jnp.float32)
        later = (even + uneven) * unit
        earlier = (even - uneven) * unit
        lane = lax.broadcasted_iota(jnp.int32, (batch * width, 128), 1)
        last = (2 * LAG - PLUS) % 128
        mirror = (last - lane) & 127
        turned = [
            jnp.take_along_axis(earlier[:, q * 128 : (q + 1) * 128], mirror, axis=1)
            for q in range(LANES // 128)
        ]
        top = (2 * LAG - PLUS) // 128
        pieces = [
            jnp.where(lane <= last, turned[top - t], turned[top - 1 - t]) for t in range(PLUS // 128)
        ]
        lagged = jnp.concatenate(pieces + [later[:, : NLAG - PLUS]], axis=1)
        lagged = lagged.reshape(batch, width, NLAG)
        if hop_index == 0:
            channel = lax.broadcasted_iota(jnp.int32, lagged.shape, 0) + step * batch
            partner = lax.broadcasted_iota(jnp.int32, lagged.shape, 1)
            lagged = jnp.where(channel == partner, 0.0, lagged)
        channels = slice(step * batch, (step + 1) * batch)
        done[channels] = lagged.astype(jnp.bfloat16)
        copy = pltpu.make_async_copy(
            done.at[channels],
            out_ref.at[channels, hop_ref[0], begin : begin + width],
            sems.at[step],
        )
        copy.start()
        copies.append(copy)
    for copy in copies:
        copy.wait()


def correlate(own, others, inverse, hop, result, begin=0):
    rec_count = own.shape[0]
    full = rec_count // NWIN
    rows = sum(other.shape[0] for other in others)
    width = rows // NWIN
    group = 8
    batch = 256 // width
    operands = [jnp.asarray(hop, jnp.int32).reshape(1), own, *others, *inverse]
    in_specs = [pl.BlockSpec(memory_space=pltpu.SMEM)]
    in_specs += [pl.BlockSpec(memory_space=pltpu.VMEM)] * (len(operands) - 1)
    aliases = {}
    if result is not None:
        in_specs.append(pl.BlockSpec(memory_space=pl.ANY))
        aliases = {len(operands): 0}
        operands.append(result)
    pairs = full * width
    return pl.pallas_call(
        functools.partial(
            correlate_kernel, hop if isinstance(hop, int) else None, begin, group, batch, len(others)
        ),
        in_specs=in_specs,
        out_specs=pl.BlockSpec(memory_space=pl.ANY),
        out_shape=jax.ShapeDtypeStruct((full, HOPS + 1, full, NLAG), jnp.bfloat16),
        scratch_shapes=[
            pltpu.VMEM((3, rec_count, F), jnp.float32),
            pltpu.VMEM((3, rows, F), jnp.float32),
            pltpu.VMEM((pairs, 2 * F), jnp.bfloat16),
            pltpu.VMEM((full, width, NLAG), jnp.bfloat16),
            pltpu.SemaphoreType.DMA((full // batch,)),
        ],
        input_output_aliases=aliases,
        compiler_params=pltpu.CompilerParams(vmem_limit_bytes=24 * MIB),
        cost_estimate=pl.CostEstimate(
            flops=pairs * 2 * F * NLAG * 4, bytes_accessed=pairs * NLAG * 2, transcendentals=0
        ),
        name="correlate",
    )(*operands)


def on_device(traces, record_id):
    rec_count = traces.shape[0]
    peers = lax.axis_size("blk")
    capacity = 2 * rec_count // peers
    slots = peers * capacity
    outgoing = spectra(traces, record_id, capacity, slots)
    width = outgoing.shape[1]
    arrived = lax.all_to_all(
        outgoing.reshape(peers, capacity // PACK, width), "blk", split_axis=0, concat_axis=0, tiled=True
    )
    arrived, inverse = lax.optimization_barrier((arrived, inverse_table()))
    own, low, high = place(arrived.reshape(slots // PACK, width), rec_count)

    odd = lax.axis_index("blk") % 2
    near_hop, far_hop = 1 + 2 * odd, 3 - 2 * odd
    barrier = lax.optimization_barrier
    side = rec_count // NWIN // 2
    low = moved(low, lambda i: i + 2)
    high = moved(high, lambda i: i + 1 if i % 2 else i + 3)
    result = correlate(own, [own], inverse, 0, None)
    low, result = barrier((low, result))
    far_low = moved(low, lambda i: i ^ 1)
    result = correlate(own, [low], inverse, 2, result)
    again, high, result = barrier((own, high, result))
    near = moved(again, lambda i: i + 3 if i % 2 else i + 1)
    far_high = moved(high, lambda i: i ^ 1)
    result = correlate(own, [high], inverse, far_hop, result, side)
    far_low, result = barrier((far_low, result))
    result = correlate(own, [far_low], inverse, far_hop, result)
    near, result = barrier((near, result))
    result = correlate(own, [near], inverse, near_hop, result)
    far_high, result = barrier((far_high, result))
    return correlate(own, [far_high], inverse, 2, result, side)


def solution(mesh):
    return jax.shard_map(
        on_device,
        mesh=mesh,
        in_specs=(P(("groups", "blk"), None), P(("groups", "blk"))),
        out_specs=P(("groups", "blk"), None, None, None),
        check_vma=False,
    )
```

```python
import functools
import math

import jax
import jax.numpy as jnp
import numpy as np
from jax import lax
from jax.experimental import pallas as pl
from jax.experimental.pallas import tpu as pltpu
from jax.sharding import PartitionSpec as P

NWIN = 8
WS = 12000
F = 512
LOWBIN = 60
LAG = 400
HOPS = 3
NLAG = 2 * LAG + 1
QUARTER = WS // 4
ENDS = (512, 1536, QUARTER)
PADDED = -(-QUARTER // 128) * 128
PLUS = 384
LANES = 512
FOURTH = F // 4
BINS = np.concatenate([LOWBIN + np.arange((m - LOWBIN) % 4, F, 4) for m in (0, 2, 1, 3)])
PACK = 4
TAIL = 128
MIB = 1024 * 1024


def moved(block, source_of):
    count = lax.axis_size("blk")
    return lax.ppermute(block, "blk", [(source_of(i) % count, i) for i in range(count)])


def inverse_table():
    bin_index = jnp.asarray(BINS, jnp.int32)[:, None]
    lag_index = jnp.arange(LANES, dtype=jnp.int32)[None, :] - (LAG - PLUS) + WS
    residue = (bin_index * lag_index % WS).astype(jnp.float32)
    angles = 2.0 * math.pi / WS * residue
    return jnp.cos(angles).astype(jnp.bfloat16), (-jnp.sin(angles)).astype(jnp.bfloat16)


def forward_table():
    angles = 2.0 * np.pi / WS * (BINS[:, None] * np.arange(QUARTER)[None, :] % WS)
    even, odd = np.split(angles, 2)
    table = np.zeros((2 * F, PADDED), np.float32)
    table[:, :QUARTER] = np.concatenate([np.cos(even), -np.sin(even), np.cos(odd), -np.sin(odd)])
    return table.astype(jnp.bfloat16)


def spectrum_kernel(capacity, id_ref, x_ref, table_ref, out_ref, samples, table, even, odd, sems):
    begins = (0,) + ENDS[:-1]
    copies = []
    for c, (begin, end) in enumerate(zip(begins, ENDS)):
        lanes = slice(begin, end if end < QUARTER else PADDED)
        pairs = [(table_ref.at[:, lanes], table.at[:, lanes])]
        for j in range(4):
            source = x_ref.at[j * QUARTER + begin : j * QUARTER + end, :]
            pairs.append((source, samples.at[j, begin:end, :]))
        copies.append(
            [pltpu.make_async_copy(a, b, sems.at[c, i]) for i, (a, b) in enumerate(pairs)]
        )
    for group in copies:
        for copy in group:
            copy.start()
    rec_count = id_ref.shape[1]
    ids = id_ref[...]
    owner = ids // rec_count
    row = jnp.broadcast_to(owner, (rec_count, rec_count))
    before = lax.broadcasted_iota(jnp.int32, row.shape, 0) < lax.broadcasted_iota(
        jnp.int32, row.shape, 1
    )
    rank = jnp.sum(jnp.where((row == row.T) & before, 1, 0), axis=0, keepdims=True)
    target = owner * capacity + rank
    label = (ids % rec_count + 1).astype(jnp.float32)
    out_rows = out_ref.shape[0]
    slot = lax.broadcasted_iota(jnp.int32, (out_rows, rec_count), 0) * PACK
    lane = lax.broadcasted_iota(jnp.int32, (out_rows, TAIL), 1)
    labels = jnp.zeros((out_rows, TAIL), jnp.float32)
    picks = []
    for q in range(PACK):
        hit = slot + q == target
        labels = jnp.where(
            lane == q, jnp.sum(jnp.where(hit, label, 0.0), axis=1, keepdims=True), labels
        )
        picks.append(jnp.where(hit, 1.0, 0.0).astype(jnp.bfloat16))
    pick = jnp.concatenate(picks)
    out_ref[:, PACK * 2 * F :] = labels.astype(jnp.bfloat16)
    for group, begin, end in zip(copies, begins, ENDS):
        for copy in group:
            copy.wait()
        for turn, total in enumerate((even, odd)):
            rows = slice(turn * F, (turn + 1) * F)
            parts = [
                jnp.dot(
                    table[rows, begin:end],
                    samples[j, begin:end, :],
                    preferred_element_type=jnp.float32,
                )
                for j in range(4)
            ]
            if turn == 0:
                straight, across = parts[0] + parts[2], parts[1] + parts[3]
                signs, order = (1, -1, 1, -1), (0, 1, 2, 3)
            else:
                straight, across = parts[0] - parts[2], parts[1] - parts[3]
                signs, order = (1, -1, -1, 1), (2, 3, 0, 1)
            for block in range(4):
                mine = slice(block * FOURTH, (block + 1) * FOURTH)
                theirs = slice(order[block] * FOURTH, (order[block] + 1) * FOURTH)
                both = straight[mine] + across[theirs] if signs[block] > 0 else straight[mine] - across[theirs]
                total[mine, :] = both if begin == 0 else total[mine, :] + both

    power = jnp.sum(even[...] * even[...], axis=0, keepdims=True)
    power = (power + jnp.sum(odd[...] * odd[...], axis=0, keepdims=True)) / F
    scale = lax.rsqrt(power + 1e-06)
    half = F // 2
    for place, (part, base) in enumerate(((even, 0), (odd, 0), (even, half), (odd, half))):
        white = (part[base : base + half, :] * scale).astype(jnp.bfloat16)
        moved = lax.dot_general(
            pick, white, (((1,), (1,)), ((), ())), preferred_element_type=jnp.float32
        ).astype(jnp.bfloat16)
        for q in range(PACK):
            lanes = slice(q * 2 * F + place * half, q * 2 * F + (place + 1) * half)
            out_ref[:, lanes] = moved[q * out_rows : (q + 1) * out_rows]


def spectra(traces, record_id, capacity, slots):
    rec_count = traces.shape[0]
    shape = (slots // PACK, PACK * 2 * F + TAIL)
    return pl.pallas_call(
        functools.partial(spectrum_kernel, capacity),
        in_specs=[
            pl.BlockSpec(memory_space=pltpu.VMEM),
            pl.BlockSpec(memory_space=pl.ANY),
            pl.BlockSpec(memory_space=pl.ANY),
        ],
        out_specs=pl.BlockSpec(memory_space=pltpu.VMEM),
        out_shape=jax.ShapeDtypeStruct(shape, jnp.bfloat16),
        scratch_shapes=[
            pltpu.VMEM((4, QUARTER, rec_count), jnp.bfloat16),
            pltpu.VMEM((2 * F, PADDED), jnp.bfloat16),
            pltpu.VMEM((F, rec_count), jnp.float32),
            pltpu.VMEM((F, rec_count), jnp.float32),
            pltpu.SemaphoreType.DMA((len(ENDS), 5)),
        ],
        compiler_params=pltpu.CompilerParams(vmem_limit_bytes=56 * MIB),
        cost_estimate=pl.CostEstimate(
            flops=4 * rec_count * WS * F, bytes_accessed=2 * WS * (rec_count + F), transcendentals=0
        ),
        name="spectra",
    )(record_id.reshape(1, rec_count), traces.T, jnp.asarray(forward_table()))


def place_kernel(arrived_ref, out_ref, *half_refs):
    rec_count = out_ref.shape[0]
    rows = arrived_ref.shape[0]
    side = rec_count // NWIN // 2
    labels = arrived_ref[:, PACK * 2 * F :].astype(jnp.float32).T.astype(jnp.int32) - 1
    want = lax.broadcasted_iota(jnp.int32, (rec_count, rows), 0)
    total = None
    for q in range(PACK):
        label = labels[q : q + 1, :]
        channel, window = label // NWIN, label % NWIN
        row = (channel // side * NWIN + window) * side + channel % side
        pick = jnp.where(want == jnp.where(label >= 0, row, -1), 1.0, 0.0).astype(jnp.bfloat16)
        part = jnp.dot(
            pick,
            arrived_ref[:, q * 2 * F : (q + 1) * 2 * F],
            preferred_element_type=jnp.float32,
        )
        total = part if q == 0 else total + part
    panel = total.astype(jnp.bfloat16)
    out_ref[...] = panel
    for half, ref in enumerate(half_refs):
        ref[...] = panel[half * rec_count // 2 : (half + 1) * rec_count // 2]


def place(arrived, rec_count):
    return pl.pallas_call(
        place_kernel,
        out_shape=[
            jax.ShapeDtypeStruct((rows, 2 * F), jnp.bfloat16)
            for rows in (rec_count, rec_count // 2, rec_count // 2)
        ],
        compiler_params=pltpu.CompilerParams(vmem_limit_bytes=8 * MIB),
        name="place",
    )(arrived)


def correlate_kernel(own_pair, spans, group, batch, count, *refs):
    hop_ref = refs[0]
    other_refs = refs[1 : 1 + count]
    cos_ref, sin_ref = refs[1 + count : 3 + count]
    if own_pair:
        out_ref, mine, theirs, cross, done, sems = refs[-6:]
    else:
        mine = refs[3 + count]
        out_ref, theirs, cross, done, sems = refs[-5:]
    full = mine.shape[1] // NWIN
    side = full // 2
    width = theirs.shape[1] // NWIN
    if len(other_refs) * side < width:
        blocks = [(other_refs[0], half * NWIN * side, half * side) for half in range(2)]
    else:
        blocks = [(ref, 0, half * side) for half, ref in enumerate(other_refs)]
    for w in range(NWIN):
        for ref, base, place in blocks:
            source = slice(base + w * side, base + (w + 1) * side)
            rows = slice(w * width + place, w * width + place + side)
            real = ref[source, :F].astype(jnp.float32)
            imag = ref[source, F:].astype(jnp.float32)
            theirs[0, rows, :] = real
            theirs[1, rows, :] = real + imag
            theirs[2, rows, :] = real - imag
            if own_pair:
                mine[0, rows, :] = real + imag
                mine[1, rows, :] = real
                mine[2, rows, :] = imag

    shared = 64 // width

    def channels_from(step, carry):
        blocks = [
            pl.ds(pl.multiple_of(w * full + step * group, group), group) for w in range(NWIN)
        ]
        for tile in range(F // 128):
            lanes = slice(tile * 128, (tile + 1) * 128)
            for first in range(0, group, shared):
                total = [[None] * 3 for _ in range(shared)]
                for w in range(NWIN):
                    for j in range(3):
                        factor = theirs[j, w * width : (w + 1) * width, lanes]
                        rows = mine.at[j, blocks[w], lanes]
                        for c in range(shared):
                            term = factor * rows[first + c : first + c + 1, :]
                            total[c][j] = term if w == 0 else total[c][j] + term
                for c in range(shared):
                    rows = pl.ds(
                        pl.multiple_of((step * group + first + c) * width, width), width
                    )
                    cross[rows, tile * 128 : (tile + 1) * 128] = (
                        total[c][0] - total[c][2]
                    ).astype(jnp.bfloat16)
                    cross[rows, F + tile * 128 : F + (tile + 1) * 128] = (
                        total[c][0] - total[c][1]
                    ).astype(jnp.bfloat16)
        return carry

    lax.fori_loop(0, full // group, channels_from, 0)
    unit = 1.0 / math.sqrt(F * NWIN)
    copies = []
    for step in range(full // batch):
        mine_rows = slice(step * batch * width, (step + 1) * batch * width)
        even = jnp.dot(cross[mine_rows, :F], cos_ref[...], preferred_element_type=jnp.float32)
        uneven = jnp.dot(cross[mine_rows, F:], sin_ref[...], preferred_element_type=jnp.float32)
        later = (even + uneven) * unit
        earlier = (even - uneven) * unit
        lane = lax.broadcasted_iota(jnp.int32, (batch * width, 128), 1)
        last = (2 * LAG - PLUS) % 128
        mirror = (last - lane) & 127
        turned = [
            jnp.take_along_axis(earlier[:, q * 128 : (q + 1) * 128], mirror, axis=1)
            for q in range(LANES // 128)
        ]
        top = (2 * LAG - PLUS) // 128
        pieces = [
            jnp.where(lane <= last, turned[top - t], turned[top - 1 - t]) for t in range(PLUS // 128)
        ]
        lagged = jnp.concatenate(pieces + [later[:, : NLAG - PLUS]], axis=1)
        lagged = lagged.reshape(batch, width, NLAG)
        if own_pair:
            channel = lax.broadcasted_iota(jnp.int32, lagged.shape, 0) + step * batch
            partner = lax.broadcasted_iota(jnp.int32, lagged.shape, 1)
            lagged = jnp.where(channel == partner, 0.0, lagged)
        channels = slice(step * batch, (step + 1) * batch)
        done[channels] = lagged.astype(jnp.bfloat16)
        for k, (hop, begin, start, length) in enumerate(spans):
            copy = pltpu.make_async_copy(
                done.at[channels, start : start + length],
                out_ref.at[channels, hop_ref[0] if hop is None else hop, begin : begin + length],
                sems.at[step, k],
            )
            copy.start()
            copies.append(copy)
    for copy in copies:
        copy.wait()


def correlate(mine, others, inverse, hop, spans, result):
    own_pair = mine is None
    rows = sum(other.shape[0] for other in others)
    width = rows // NWIN
    form = jax.ShapeDtypeStruct((3, rows, F), jnp.float32) if own_pair else mine
    full = form.shape[1] // NWIN
    group = 8
    batch = 256 // width
    operands = [jnp.asarray(hop, jnp.int32).reshape(1), *others, *inverse]
    if not own_pair:
        operands.append(mine)
    in_specs = [pl.BlockSpec(memory_space=pltpu.SMEM)]
    in_specs += [pl.BlockSpec(memory_space=pltpu.VMEM)] * (len(operands) - 1)
    out_specs = [pl.BlockSpec(memory_space=pl.ANY)]
    out_shape = [jax.ShapeDtypeStruct((full, HOPS + 1, full, NLAG), jnp.bfloat16)]
    aliases = {}
    if own_pair:
        out_specs.append(pl.BlockSpec(memory_space=pltpu.VMEM))
        out_shape.append(form)
    else:
        in_specs.append(pl.BlockSpec(memory_space=pl.ANY))
        aliases = {len(operands): 0}
        operands.append(result)
    pairs = full * width
    return pl.pallas_call(
        functools.partial(correlate_kernel, own_pair, spans, group, batch, len(others)),
        in_specs=in_specs,
        out_specs=out_specs,
        out_shape=out_shape,
        scratch_shapes=[
            pltpu.VMEM((3, rows, F), jnp.float32),
            pltpu.VMEM((pairs, 2 * F), jnp.bfloat16),
            pltpu.VMEM((full, width, NLAG), jnp.bfloat16),
            pltpu.SemaphoreType.DMA((full // batch, len(spans))),
        ],
        input_output_aliases=aliases,
        compiler_params=pltpu.CompilerParams(vmem_limit_bytes=24 * MIB),
        cost_estimate=pl.CostEstimate(
            flops=pairs * 2 * F * NLAG * 4, bytes_accessed=pairs * NLAG * 2, transcendentals=0
        ),
        name="correlate",
    )(*operands)


def on_device(traces, record_id):
    rec_count = traces.shape[0]
    peers = lax.axis_size("blk")
    capacity = 2 * rec_count // peers
    slots = peers * capacity
    outgoing = spectra(traces, record_id, capacity, slots)
    width = outgoing.shape[1]
    arrived = lax.all_to_all(
        outgoing.reshape(peers, capacity // PACK, width), "blk", split_axis=0, concat_axis=0, tiled=True
    )
    arrived, inverse = lax.optimization_barrier((arrived, inverse_table()))
    own, low, high = place(arrived.reshape(slots // PACK, width), rec_count)

    odd = lax.axis_index("blk") % 2
    near_hop, far_hop = 1 + 2 * odd, 3 - 2 * odd
    barrier = lax.optimization_barrier
    side = rec_count // NWIN // 2
    low = moved(low, lambda i: i + 2)
    high = moved(high, lambda i: i + 1 if i % 2 else i + 3)
    whole, first = (None, 0, 0, 2 * side), (None, 0, 0, side)
    result, mine = correlate(None, [own], inverse, 0, (whole,), None)

    def add(others, hop, *spans):
        return correlate(mine, others, inverse, hop, spans, result)[0]

    low, result = barrier((low, result))
    far_low = moved(low, lambda i: i ^ 1)
    result = add([low], 2, first)
    again, high, result = barrier((own, high, result))
    near = moved(again, lambda i: i + 3 if i % 2 else i + 1)
    far_high = moved(high, lambda i: i ^ 1)
    result = add([high], far_hop, (None, side, 0, side))
    near, result = barrier((near, result))
    result = add([near], near_hop, whole)
    far_low, far_high, result = barrier((far_low, far_high, result))
    return add([far_low, far_high], far_hop, first, (2, side, side, side))


def solution(mesh):
    return jax.shard_map(
        on_device,
        mesh=mesh,
        in_specs=(P(("groups", "blk"), None), P(("groups", "blk"))),
        out_specs=P(("groups", "blk"), None, None, None),
        check_vma=False,
    )
```

```python
import functools
import math

import jax
import jax.numpy as jnp
import numpy as np
from jax import lax
from jax.experimental import pallas as pl
from jax.experimental.pallas import tpu as pltpu
from jax.sharding import PartitionSpec as P

NWIN = 8
WS = 12000
F = 512
LOWBIN = 60
LAG = 400
HOPS = 3
NLAG = 2 * LAG + 1
QUARTER = WS // 4
ENDS = (512, 1536, QUARTER)
PADDED = -(-QUARTER // 128) * 128
PLUS = 384
LANES = 512
FOURTH = F // 4
BINS = np.concatenate([LOWBIN + np.arange((m - LOWBIN) % 4, F, 4) for m in (0, 2, 1, 3)])
PACK = 4
TAIL = 128
MIB = 1024 * 1024


def moved(block, source_of):
    count = lax.axis_size("blk")
    return lax.ppermute(block, "blk", [(source_of(i) % count, i) for i in range(count)])


def inverse_table():
    bin_index = jnp.asarray(BINS, jnp.int32)[:, None]
    lag_index = jnp.arange(LANES, dtype=jnp.int32)[None, :] - (LAG - PLUS) + WS
    residue = (bin_index * lag_index % WS).astype(jnp.float32)
    angles = 2.0 * math.pi / WS * residue
    return jnp.cos(angles).astype(jnp.bfloat16), (-jnp.sin(angles)).astype(jnp.bfloat16)


def forward_table():
    angles = 2.0 * np.pi / WS * (BINS[:, None] * np.arange(QUARTER)[None, :] % WS)
    even, odd = np.split(angles, 2)
    table = np.zeros((2 * F, PADDED), np.float32)
    table[:, :QUARTER] = np.concatenate([np.cos(even), -np.sin(even), np.cos(odd), -np.sin(odd)])
    return table.astype(jnp.bfloat16)


def spectrum_kernel(capacity, id_ref, x_ref, table_ref, out_ref, samples, table, even, odd, sems):
    begins = (0,) + ENDS[:-1]
    copies = []
    for c, (begin, end) in enumerate(zip(begins, ENDS)):
        lanes = slice(begin, end if end < QUARTER else PADDED)
        pairs = [(table_ref.at[:, lanes], table.at[:, lanes])]
        for j in range(4):
            source = x_ref.at[j * QUARTER + begin : j * QUARTER + end, :]
            pairs.append((source, samples.at[j, begin:end, :]))
        copies.append(
            [pltpu.make_async_copy(a, b, sems.at[c, i]) for i, (a, b) in enumerate(pairs)]
        )
    for group in copies:
        for copy in group:
            copy.start()
    rec_count = id_ref.shape[1]
    ids = id_ref[...]
    owner = ids // rec_count
    row = jnp.broadcast_to(owner, (rec_count, rec_count))
    before = lax.broadcasted_iota(jnp.int32, row.shape, 0) < lax.broadcasted_iota(
        jnp.int32, row.shape, 1
    )
    rank = jnp.sum(jnp.where((row == row.T) & before, 1, 0), axis=0, keepdims=True)
    target = owner * capacity + rank
    label = (ids % rec_count + 1).astype(jnp.float32)
    out_rows = out_ref.shape[0]
    slot = lax.broadcasted_iota(jnp.int32, (out_rows, rec_count), 0) * PACK
    lane = lax.broadcasted_iota(jnp.int32, (out_rows, TAIL), 1)
    labels = jnp.zeros((out_rows, TAIL), jnp.float32)
    picks = []
    for q in range(PACK):
        hit = slot + q == target
        labels = jnp.where(
            lane == q, jnp.sum(jnp.where(hit, label, 0.0), axis=1, keepdims=True), labels
        )
        picks.append(jnp.where(hit, 1.0, 0.0).astype(jnp.bfloat16))
    pick = jnp.concatenate(picks)
    out_ref[:, PACK * 2 * F :] = labels.astype(jnp.bfloat16)
    for group, begin, end in zip(copies, begins, ENDS):
        for copy in group:
            copy.wait()
        for turn, total in enumerate((even, odd)):
            rows = slice(turn * F, (turn + 1) * F)
            parts = [
                jnp.dot(
                    table[rows, begin:end],
                    samples[j, begin:end, :],
                    preferred_element_type=jnp.float32,
                )
                for j in range(4)
            ]
            if turn == 0:
                straight, across = parts[0] + parts[2], parts[1] + parts[3]
                signs, order = (1, -1, 1, -1), (0, 1, 2, 3)
            else:
                straight, across = parts[0] - parts[2], parts[1] - parts[3]
                signs, order = (1, -1, -1, 1), (2, 3, 0, 1)
            for block in range(4):
                mine = slice(block * FOURTH, (block + 1) * FOURTH)
                theirs = slice(order[block] * FOURTH, (order[block] + 1) * FOURTH)
                both = straight[mine] + across[theirs] if signs[block] > 0 else straight[mine] - across[theirs]
                total[mine, :] = both if begin == 0 else total[mine, :] + both

    power = jnp.sum(even[...] * even[...], axis=0, keepdims=True)
    power = (power + jnp.sum(odd[...] * odd[...], axis=0, keepdims=True)) / F
    scale = lax.rsqrt(power + 1e-06)
    half = F // 2
    for place, (part, base) in enumerate(((even, 0), (odd, 0), (even, half), (odd, half))):
        white = (part[base : base + half, :] * scale).astype(jnp.bfloat16)
        moved = lax.dot_general(
            pick, white, (((1,), (1,)), ((), ())), preferred_element_type=jnp.float32
        ).astype(jnp.bfloat16)
        for q in range(PACK):
            lanes = slice(q * 2 * F + place * half, q * 2 * F + (place + 1) * half)
            out_ref[:, lanes] = moved[q * out_rows : (q + 1) * out_rows]


def spectra(traces, record_id, capacity, slots):
    rec_count = traces.shape[0]
    shape = (slots // PACK, PACK * 2 * F + TAIL)
    return pl.pallas_call(
        functools.partial(spectrum_kernel, capacity),
        in_specs=[
            pl.BlockSpec(memory_space=pltpu.VMEM),
            pl.BlockSpec(memory_space=pl.ANY),
            pl.BlockSpec(memory_space=pl.ANY),
        ],
        out_specs=pl.BlockSpec(memory_space=pltpu.VMEM),
        out_shape=jax.ShapeDtypeStruct(shape, jnp.bfloat16),
        scratch_shapes=[
            pltpu.VMEM((4, QUARTER, rec_count), jnp.bfloat16),
            pltpu.VMEM((2 * F, PADDED), jnp.bfloat16),
            pltpu.VMEM((F, rec_count), jnp.float32),
            pltpu.VMEM((F, rec_count), jnp.float32),
            pltpu.SemaphoreType.DMA((len(ENDS), 5)),
        ],
        compiler_params=pltpu.CompilerParams(vmem_limit_bytes=56 * MIB),
        cost_estimate=pl.CostEstimate(
            flops=4 * rec_count * WS * F, bytes_accessed=2 * WS * (rec_count + F), transcendentals=0
        ),
        name="spectra",
    )(record_id.reshape(1, rec_count), traces.T, jnp.asarray(forward_table()))


def place_kernel(arrived_ref, out_ref, *half_refs):
    rec_count = out_ref.shape[0]
    rows = arrived_ref.shape[0]
    side = rec_count // NWIN // 2
    labels = arrived_ref[:, PACK * 2 * F :].astype(jnp.float32).T.astype(jnp.int32) - 1
    want = lax.broadcasted_iota(jnp.int32, (rec_count, rows), 0)
    total = None
    for q in range(PACK):
        label = labels[q : q + 1, :]
        channel, window = label // NWIN, label % NWIN
        row = (channel // side * NWIN + window) * side + channel % side
        pick = jnp.where(want == jnp.where(label >= 0, row, -1), 1.0, 0.0).astype(jnp.bfloat16)
        part = jnp.dot(
            pick,
            arrived_ref[:, q * 2 * F : (q + 1) * 2 * F],
            preferred_element_type=jnp.float32,
        )
        total = part if q == 0 else total + part
    panel = total.astype(jnp.bfloat16)
    out_ref[...] = panel
    for half, ref in enumerate(half_refs):
        ref[...] = panel[half * rec_count // 2 : (half + 1) * rec_count // 2]


def place(arrived, rec_count):
    return pl.pallas_call(
        place_kernel,
        out_shape=[
            jax.ShapeDtypeStruct((rows, 2 * F), jnp.bfloat16)
            for rows in (rec_count, rec_count // 2, rec_count // 2)
        ],
        compiler_params=pltpu.CompilerParams(vmem_limit_bytes=8 * MIB),
        name="place",
    )(arrived)


def correlate_kernel(own_pair, spans, group, batch, count, *refs):
    hop_ref, own_ref = refs[:2]
    other_refs = refs[2 : 2 + count]
    cos_ref, sin_ref = refs[2 + count : 4 + count]
    out_ref, mine, theirs, cross, done, sems = refs[-6:]
    full = mine.shape[1] // NWIN
    side = full // 2
    width = theirs.shape[1] // NWIN
    own_blocks = [(own_ref, half * NWIN * side, half * side) for half in range(2)]
    if len(other_refs) * side < width:
        blocks = [(other_refs[0], half * NWIN * side, half * side) for half in range(2)]
    else:
        blocks = [(ref, 0, half * side) for half, ref in enumerate(other_refs)]
    for w in range(NWIN):
        for ref, base, place in own_blocks:
            source = slice(base + w * side, base + (w + 1) * side)
            rows = slice(w * full + place, w * full + place + side)
            real = ref[source, :F].astype(jnp.float32)
            imag = ref[source, F:].astype(jnp.float32)
            mine[0, rows, :] = real + imag
            mine[1, rows, :] = real
            mine[2, rows, :] = imag
        for ref, base, place in blocks:
            source = slice(base + w * side, base + (w + 1) * side)
            rows = slice(w * width + place, w * width + place + side)
            real = ref[source, :F].astype(jnp.float32)
            imag = ref[source, F:].astype(jnp.float32)
            theirs[0, rows, :] = real
            theirs[1, rows, :] = real + imag
            theirs[2, rows, :] = real - imag

    shared = 64 // width

    def channels_from(step, carry):
        blocks = [
            pl.ds(pl.multiple_of(w * full + step * group, group), group) for w in range(NWIN)
        ]
        for tile in range(F // 128):
            lanes = slice(tile * 128, (tile + 1) * 128)
            for first in range(0, group, shared):
                total = [[None] * 3 for _ in range(shared)]
                for w in range(NWIN):
                    for j in range(3):
                        factor = theirs[j, w * width : (w + 1) * width, lanes]
                        rows = mine.at[j, blocks[w], lanes]
                        for c in range(shared):
                            term = factor * rows[first + c : first + c + 1, :]
                            total[c][j] = term if w == 0 else total[c][j] + term
                for c in range(shared):
                    rows = pl.ds(
                        pl.multiple_of((step * group + first + c) * width, width), width
                    )
                    cross[rows, tile * 128 : (tile + 1) * 128] = (
                        total[c][0] - total[c][2]
                    ).astype(jnp.bfloat16)
                    cross[rows, F + tile * 128 : F + (tile + 1) * 128] = (
                        total[c][0] - total[c][1]
                    ).astype(jnp.bfloat16)
        return carry

    lax.fori_loop(0, full // group, channels_from, 0)
    unit = 1.0 / math.sqrt(F * NWIN)
    copies = []
    for step in range(full // batch):
        mine_rows = slice(step * batch * width, (step + 1) * batch * width)
        even = jnp.dot(cross[mine_rows, :F], cos_ref[...], preferred_element_type=jnp.float32)
        uneven = jnp.dot(cross[mine_rows, F:], sin_ref[...], preferred_element_type=jnp.float32)
        later = (even + uneven) * unit
        earlier = (even - uneven) * unit
        lane = lax.broadcasted_iota(jnp.int32, (batch * width, 128), 1)
        last = (2 * LAG - PLUS) % 128
        mirror = (last - lane) & 127
        turned = [
            jnp.take_along_axis(earlier[:, q * 128 : (q + 1) * 128], mirror, axis=1)
            for q in range(LANES // 128)
        ]
        top = (2 * LAG - PLUS) // 128
        pieces = [
            jnp.where(lane <= last, turned[top - t], turned[top - 1 - t]) for t in range(PLUS // 128)
        ]
        lagged = jnp.concatenate(pieces + [later[:, : NLAG - PLUS]], axis=1)
        lagged = lagged.reshape(batch, width, NLAG)
        if own_pair:
            channel = lax.broadcasted_iota(jnp.int32, lagged.shape, 0) + step * batch
            partner = lax.broadcasted_iota(jnp.int32, lagged.shape, 1) + spans[0][1]
            lagged = jnp.where(channel == partner, 0.0, lagged)
        channels = slice(step * batch, (step + 1) * batch)
        done[channels] = lagged.astype(jnp.bfloat16)
        for k, (hop, begin, start, length) in enumerate(spans):
            copy = pltpu.make_async_copy(
                done.at[channels, start : start + length],
                out_ref.at[channels, hop_ref[0] if hop is None else hop, begin : begin + length],
                sems.at[step, k],
            )
            copy.start()
            copies.append(copy)
    for copy in copies:
        copy.wait()


def correlate(own, others, inverse, hop, spans, result, own_pair=False):
    rows = sum(other.shape[0] for other in others)
    width = rows // NWIN
    full = own.shape[0] // NWIN
    group = 8
    batch = 256 // width
    operands = [jnp.asarray(hop, jnp.int32).reshape(1), own, *others, *inverse]
    in_specs = [pl.BlockSpec(memory_space=pltpu.SMEM)]
    in_specs += [pl.BlockSpec(memory_space=pltpu.VMEM)] * (len(operands) - 1)
    aliases = {}
    if result is not None:
        in_specs.append(pl.BlockSpec(memory_space=pl.ANY))
        aliases = {len(operands): 0}
        operands.append(result)
    pairs = full * width
    return pl.pallas_call(
        functools.partial(correlate_kernel, own_pair, spans, group, batch, len(others)),
        in_specs=in_specs,
        out_specs=pl.BlockSpec(memory_space=pl.ANY),
        out_shape=jax.ShapeDtypeStruct((full, HOPS + 1, full, NLAG), jnp.bfloat16),
        scratch_shapes=[
            pltpu.VMEM((3, own.shape[0], F), jnp.float32),
            pltpu.VMEM((3, rows, F), jnp.float32),
            pltpu.VMEM((pairs, 2 * F), jnp.bfloat16),
            pltpu.VMEM((full, width, NLAG), jnp.bfloat16),
            pltpu.SemaphoreType.DMA((full // batch, len(spans))),
        ],
        input_output_aliases=aliases,
        compiler_params=pltpu.CompilerParams(vmem_limit_bytes=24 * MIB),
        cost_estimate=pl.CostEstimate(
            flops=pairs * 2 * F * NLAG * 4, bytes_accessed=pairs * NLAG * 2, transcendentals=0
        ),
        name="correlate",
    )(*operands)


def on_device(traces, record_id):
    rec_count = traces.shape[0]
    peers = lax.axis_size("blk")
    capacity = 2 * rec_count // peers
    slots = peers * capacity
    outgoing = spectra(traces, record_id, capacity, slots)
    width = outgoing.shape[1]
    arrived = lax.all_to_all(
        outgoing.reshape(peers, capacity // PACK, width), "blk", split_axis=0, concat_axis=0, tiled=True
    )
    arrived, inverse = lax.optimization_barrier((arrived, inverse_table()))
    own, low, high = place(arrived.reshape(slots // PACK, width), rec_count)

    odd = lax.axis_index("blk") % 2
    near_hop, far_hop = 1 + 2 * odd, 3 - 2 * odd
    barrier = lax.optimization_barrier
    side = rec_count // NWIN // 2
    whole, first, second = (None, 0, 0, 2 * side), (None, 0, 0, side), (None, side, 0, side)

    def add(others, hop, *spans, own_pair=False):
        return correlate(own, others, inverse, hop, spans, result, own_pair)

    result = None
    low = moved(low, lambda i: i + 2)
    high = moved(high, lambda i: i + 1 if i % 2 else i + 3)
    result = add([own], 0, whole, own_pair=True)
    low, result = barrier((low, result))
    far_low = moved(low, lambda i: i ^ 1)
    result = add([low], 2, first)
    again, high, result = barrier((own, high, result))
    near = moved(again, lambda i: i + 3 if i % 2 else i + 1)
    far_high = moved(high, lambda i: i ^ 1)
    result = add([high], far_hop, second)
    far_low, far_high, result = barrier((far_low, far_high, result))
    result = add([far_low, far_high], far_hop, first, (2, side, side, side))
    near, result = barrier((near, result))
    return add([near], near_hop, whole)


def solution(mesh):
    return jax.shard_map(
        on_device,
        mesh=mesh,
        in_specs=(P(("groups", "blk"), None), P(("groups", "blk"))),
        out_specs=P(("groups", "blk"), None, None, None),
        check_vma=False,
    )
```

```python
import functools
import math

import jax
import jax.numpy as jnp
import numpy as np
from jax import lax
from jax.experimental import pallas as pl
from jax.experimental.pallas import tpu as pltpu
from jax.sharding import PartitionSpec as P

NWIN = 8
WS = 12000
F = 512
LOWBIN = 60
LAG = 400
HOPS = 3
NLAG = 2 * LAG + 1
QUARTER = WS // 4
ENDS = (512, 1536, QUARTER)
PADDED = -(-QUARTER // 128) * 128
PLUS = 384
LANES = 512
FOURTH = F // 4
BINS = np.concatenate([LOWBIN + np.arange((m - LOWBIN) % 4, F, 4) for m in (0, 2, 1, 3)])
PACK = 4
TAIL = 128
MIB = 1024 * 1024


def moved(block, source_of):
    count = lax.axis_size("blk")
    return lax.ppermute(block, "blk", [(source_of(i) % count, i) for i in range(count)])


def inverse_table():
    bin_index = jnp.asarray(BINS, jnp.int32)[:, None]
    lag_index = jnp.arange(LANES, dtype=jnp.int32)[None, :] - (LAG - PLUS) + WS
    residue = (bin_index * lag_index % WS).astype(jnp.float32)
    angles = 2.0 * math.pi / WS * residue
    return jnp.cos(angles).astype(jnp.bfloat16), (-jnp.sin(angles)).astype(jnp.bfloat16)


def forward_table():
    angles = 2.0 * np.pi / WS * (BINS[:, None] * np.arange(QUARTER)[None, :] % WS)
    even, odd = np.split(angles, 2)
    table = np.zeros((2 * F, PADDED), np.float32)
    table[:, :QUARTER] = np.concatenate([np.cos(even), -np.sin(even), np.cos(odd), -np.sin(odd)])
    return table.astype(jnp.bfloat16)


def spectrum_kernel(capacity, id_ref, x_ref, table_ref, out_ref, samples, table, even, odd, sems):
    begins = (0,) + ENDS[:-1]
    copies = []
    for c, (begin, end) in enumerate(zip(begins, ENDS)):
        lanes = slice(begin, end if end < QUARTER else PADDED)
        pairs = [(table_ref.at[:, lanes], table.at[:, lanes])]
        for j in range(4):
            source = x_ref.at[j * QUARTER + begin : j * QUARTER + end, :]
            pairs.append((source, samples.at[j, begin:end, :]))
        copies.append(
            [pltpu.make_async_copy(a, b, sems.at[c, i]) for i, (a, b) in enumerate(pairs)]
        )
    for group in copies:
        for copy in group:
            copy.start()
    rec_count = id_ref.shape[1]
    ids = id_ref[...]
    owner = ids // rec_count
    row = jnp.broadcast_to(owner, (rec_count, rec_count))
    before = lax.broadcasted_iota(jnp.int32, row.shape, 0) < lax.broadcasted_iota(
        jnp.int32, row.shape, 1
    )
    rank = jnp.sum(jnp.where((row == row.T) & before, 1, 0), axis=0, keepdims=True)
    target = owner * capacity + rank
    label = (ids % rec_count + 1).astype(jnp.float32)
    out_rows = out_ref.shape[0]
    slot = lax.broadcasted_iota(jnp.int32, (out_rows, rec_count), 0) * PACK
    lane = lax.broadcasted_iota(jnp.int32, (out_rows, TAIL), 1)
    labels = jnp.zeros((out_rows, TAIL), jnp.float32)
    picks = []
    for q in range(PACK):
        hit = slot + q == target
        labels = jnp.where(
            lane == q, jnp.sum(jnp.where(hit, label, 0.0), axis=1, keepdims=True), labels
        )
        picks.append(jnp.where(hit, 1.0, 0.0).astype(jnp.bfloat16))
    pick = jnp.concatenate(picks)
    out_ref[:, PACK * 2 * F :] = labels.astype(jnp.bfloat16)
    for group, begin, end in zip(copies, begins, ENDS):
        for copy in group:
            copy.wait()
        for turn, total in enumerate((even, odd)):
            rows = slice(turn * F, (turn + 1) * F)
            parts = [
                jnp.dot(
                    table[rows, begin:end],
                    samples[j, begin:end, :],
                    preferred_element_type=jnp.float32,
                )
                for j in range(4)
            ]
            if turn == 0:
                straight, across = parts[0] + parts[2], parts[1] + parts[3]
                signs, order = (1, -1, 1, -1), (0, 1, 2, 3)
            else:
                straight, across = parts[0] - parts[2], parts[1] - parts[3]
                signs, order = (1, -1, -1, 1), (2, 3, 0, 1)
            for block in range(4):
                mine = slice(block * FOURTH, (block + 1) * FOURTH)
                theirs = slice(order[block] * FOURTH, (order[block] + 1) * FOURTH)
                both = straight[mine] + across[theirs] if signs[block] > 0 else straight[mine] - across[theirs]
                total[mine, :] = both if begin == 0 else total[mine, :] + both

    power = jnp.sum(even[...] * even[...], axis=0, keepdims=True)
    power = (power + jnp.sum(odd[...] * odd[...], axis=0, keepdims=True)) / F
    scale = lax.rsqrt(power + 1e-06)
    half = F // 2
    for place, (part, base) in enumerate(((even, 0), (odd, 0), (even, half), (odd, half))):
        white = (part[base : base + half, :] * scale).astype(jnp.bfloat16)
        moved = lax.dot_general(
            pick, white, (((1,), (1,)), ((), ())), preferred_element_type=jnp.float32
        ).astype(jnp.bfloat16)
        for q in range(PACK):
            lanes = slice(q * 2 * F + place * half, q * 2 * F + (place + 1) * half)
            out_ref[:, lanes] = moved[q * out_rows : (q + 1) * out_rows]


def spectra(traces, record_id, capacity, slots):
    rec_count = traces.shape[0]
    shape = (slots // PACK, PACK * 2 * F + TAIL)
    return pl.pallas_call(
        functools.partial(spectrum_kernel, capacity),
        in_specs=[
            pl.BlockSpec(memory_space=pltpu.VMEM),
            pl.BlockSpec(memory_space=pl.ANY),
            pl.BlockSpec(memory_space=pl.ANY),
        ],
        out_specs=pl.BlockSpec(memory_space=pltpu.VMEM),
        out_shape=jax.ShapeDtypeStruct(shape, jnp.bfloat16),
        scratch_shapes=[
            pltpu.VMEM((4, QUARTER, rec_count), jnp.bfloat16),
            pltpu.VMEM((2 * F, PADDED), jnp.bfloat16),
            pltpu.VMEM((F, rec_count), jnp.float32),
            pltpu.VMEM((F, rec_count), jnp.float32),
            pltpu.SemaphoreType.DMA((len(ENDS), 5)),
        ],
        compiler_params=pltpu.CompilerParams(vmem_limit_bytes=56 * MIB),
        cost_estimate=pl.CostEstimate(
            flops=4 * rec_count * WS * F, bytes_accessed=2 * WS * (rec_count + F), transcendentals=0
        ),
        name="spectra",
    )(record_id.reshape(1, rec_count), traces.T, jnp.asarray(forward_table()))


def place_kernel(arrived_ref, out_ref, *half_refs):
    rec_count = out_ref.shape[0]
    rows = arrived_ref.shape[0]
    side = rec_count // NWIN // 2
    labels = arrived_ref[:, PACK * 2 * F :].astype(jnp.float32).T.astype(jnp.int32) - 1
    want = lax.broadcasted_iota(jnp.int32, (rec_count, rows), 0)
    total = None
    for q in range(PACK):
        label = labels[q : q + 1, :]
        channel, window = label // NWIN, label % NWIN
        row = (channel // side * NWIN + window) * side + channel % side
        pick = jnp.where(want == jnp.where(label >= 0, row, -1), 1.0, 0.0).astype(jnp.bfloat16)
        part = jnp.dot(
            pick,
            arrived_ref[:, q * 2 * F : (q + 1) * 2 * F],
            preferred_element_type=jnp.float32,
        )
        total = part if q == 0 else total + part
    panel = total.astype(jnp.bfloat16)
    out_ref[...] = panel
    for half, ref in enumerate(half_refs):
        ref[...] = panel[half * rec_count // 2 : (half + 1) * rec_count // 2]


def place(arrived, rec_count):
    return pl.pallas_call(
        place_kernel,
        out_shape=[
            jax.ShapeDtypeStruct((rows, 2 * F), jnp.bfloat16)
            for rows in (rec_count, rec_count // 2, rec_count // 2)
        ],
        compiler_params=pltpu.CompilerParams(vmem_limit_bytes=8 * MIB),
        name="place",
    )(arrived)


def correlate_kernel(own_pair, spans, group, batch, count, *refs):
    hop_ref, own_ref = refs[:2]
    other_refs = refs[2 : 2 + count]
    cos_ref, sin_ref = refs[2 + count : 4 + count]
    out_ref, mine, theirs, cross, done, sems = refs[-6:]
    full = mine.shape[1] // NWIN
    side = full // 2
    width = theirs.shape[1] // NWIN
    own_blocks = [(own_ref, half * NWIN * side, half * side) for half in range(2)]
    if len(other_refs) * side < width:
        blocks = [(other_refs[0], half * NWIN * side, half * side) for half in range(2)]
    else:
        blocks = [(ref, 0, half * side) for half, ref in enumerate(other_refs)]
    for w in range(NWIN):
        for ref, base, place in own_blocks:
            source = slice(base + w * side, base + (w + 1) * side)
            rows = slice(w * full + place, w * full + place + side)
            real = ref[source, :F].astype(jnp.float32)
            imag = ref[source, F:].astype(jnp.float32)
            mine[0, rows, :] = real + imag
            mine[1, rows, :] = real
            mine[2, rows, :] = imag
        for ref, base, place in blocks:
            source = slice(base + w * side, base + (w + 1) * side)
            rows = slice(w * width + place, w * width + place + side)
            real = ref[source, :F].astype(jnp.float32)
            imag = ref[source, F:].astype(jnp.float32)
            theirs[0, rows, :] = real
            theirs[1, rows, :] = real + imag
            theirs[2, rows, :] = real - imag

    shared = 4

    def channels_from(step, carry):
        blocks = [
            pl.ds(pl.multiple_of(w * full + step * group, group), group) for w in range(NWIN)
        ]
        for tile in range(F // 128):
            lanes = slice(tile * 128, (tile + 1) * 128)
            for first in range(0, group, shared):
                total = [[None] * 3 for _ in range(shared)]
                for w in range(NWIN):
                    for j in range(3):
                        factor = theirs[j, w * width : (w + 1) * width, lanes]
                        rows = mine.at[j, blocks[w], lanes]
                        for c in range(shared):
                            term = factor * rows[first + c : first + c + 1, :]
                            total[c][j] = term if w == 0 else total[c][j] + term
                for c in range(shared):
                    rows = pl.ds(
                        pl.multiple_of((step * group + first + c) * width, width), width
                    )
                    cross[rows, tile * 128 : (tile + 1) * 128] = (
                        total[c][0] - total[c][2]
                    ).astype(jnp.bfloat16)
                    cross[rows, F + tile * 128 : F + (tile + 1) * 128] = (
                        total[c][0] - total[c][1]
                    ).astype(jnp.bfloat16)
        return carry

    lax.fori_loop(0, full // group, channels_from, 0)
    unit = 1.0 / math.sqrt(F * NWIN)
    copies = []
    for step in range(full // batch):
        mine_rows = slice(step * batch * width, (step + 1) * batch * width)
        even = jnp.dot(cross[mine_rows, :F], cos_ref[...], preferred_element_type=jnp.float32)
        uneven = jnp.dot(cross[mine_rows, F:], sin_ref[...], preferred_element_type=jnp.float32)
        later = (even + uneven) * unit
        earlier = (even - uneven) * unit
        lane = lax.broadcasted_iota(jnp.int32, (batch * width, 128), 1)
        last = (2 * LAG - PLUS) % 128
        mirror = (last - lane) & 127
        turned = [
            jnp.take_along_axis(earlier[:, q * 128 : (q + 1) * 128], mirror, axis=1)
            for q in range(LANES // 128)
        ]
        top = (2 * LAG - PLUS) // 128
        pieces = [
            jnp.where(lane <= last, turned[top - t], turned[top - 1 - t]) for t in range(PLUS // 128)
        ]
        lagged = jnp.concatenate(pieces + [later[:, : NLAG - PLUS]], axis=1)
        lagged = lagged.reshape(batch, width, NLAG)
        if own_pair:
            channel = lax.broadcasted_iota(jnp.int32, lagged.shape, 0) + step * batch
            partner = lax.broadcasted_iota(jnp.int32, lagged.shape, 1) + spans[0][1]
            lagged = jnp.where(channel == partner, 0.0, lagged)
        channels = slice(step * batch, (step + 1) * batch)
        done[channels] = lagged.astype(jnp.bfloat16)
        for k, (hop, begin, start, length) in enumerate(spans):
            copy = pltpu.make_async_copy(
                done.at[channels, start : start + length],
                out_ref.at[channels, hop_ref[0] if hop is None else hop, begin : begin + length],
                sems.at[step, k],
            )
            copy.start()
            copies.append(copy)
    for copy in copies:
        copy.wait()


def correlate(own, others, inverse, hop, spans, result, own_pair=False):
    rows = sum(other.shape[0] for other in others)
    width = rows // NWIN
    full = own.shape[0] // NWIN
    group = 8
    batch = 128 // width
    operands = [jnp.asarray(hop, jnp.int32).reshape(1), own, *others, *inverse]
    in_specs = [pl.BlockSpec(memory_space=pltpu.SMEM)]
    in_specs += [pl.BlockSpec(memory_space=pltpu.VMEM)] * (len(operands) - 1)
    aliases = {}
    if result is not None:
        in_specs.append(pl.BlockSpec(memory_space=pl.ANY))
        aliases = {len(operands): 0}
        operands.append(result)
    pairs = full * width
    return pl.pallas_call(
        functools.partial(correlate_kernel, own_pair, spans, group, batch, len(others)),
        in_specs=in_specs,
        out_specs=pl.BlockSpec(memory_space=pl.ANY),
        out_shape=jax.ShapeDtypeStruct((full, HOPS + 1, full, NLAG), jnp.bfloat16),
        scratch_shapes=[
            pltpu.VMEM((3, own.shape[0], F), jnp.float32),
            pltpu.VMEM((3, rows, F), jnp.float32),
            pltpu.VMEM((pairs, 2 * F), jnp.bfloat16),
            pltpu.VMEM((full, width, NLAG), jnp.bfloat16),
            pltpu.SemaphoreType.DMA((full // batch, len(spans))),
        ],
        input_output_aliases=aliases,
        compiler_params=pltpu.CompilerParams(vmem_limit_bytes=24 * MIB),
        cost_estimate=pl.CostEstimate(
            flops=pairs * 2 * F * NLAG * 4, bytes_accessed=pairs * NLAG * 2, transcendentals=0
        ),
        name="correlate",
    )(*operands)


def on_device(traces, record_id):
    rec_count = traces.shape[0]
    peers = lax.axis_size("blk")
    capacity = 2 * rec_count // peers
    slots = peers * capacity
    outgoing = spectra(traces, record_id, capacity, slots)
    width = outgoing.shape[1]
    arrived = lax.all_to_all(
        outgoing.reshape(peers, capacity // PACK, width), "blk", split_axis=0, concat_axis=0, tiled=True
    )
    arrived, inverse = lax.optimization_barrier((arrived, inverse_table()))
    own, low, high = place(arrived.reshape(slots // PACK, width), rec_count)

    odd = lax.axis_index("blk") % 2
    near_hop, far_hop = 1 + 2 * odd, 3 - 2 * odd
    barrier = lax.optimization_barrier
    side = rec_count // NWIN // 2
    whole, first, second = (None, 0, 0, 2 * side), (None, 0, 0, side), (None, side, 0, side)

    def add(others, hop, *spans, own_pair=False):
        return correlate(own, others, inverse, hop, spans, result, own_pair)

    result = None
    low = moved(low, lambda i: i + 2)
    high = moved(high, lambda i: i + 1 if i % 2 else i + 3)
    result = add([own], 0, whole, own_pair=True)
    low, result = barrier((low, result))
    far_low = moved(low, lambda i: i ^ 1)
    result = add([low], 2, first)
    again, high, result = barrier((own, high, result))
    near = moved(again, lambda i: i + 3 if i % 2 else i + 1)
    far_high = moved(high, lambda i: i ^ 1)
    result = add([high], far_hop, second)
    far_low, far_high, result = barrier((far_low, far_high, result))
    result = add([far_low, far_high], far_hop, first, (2, side, side, side))
    near, result = barrier((near, result))
    return add([near], near_hop, whole)


def solution(mesh):
    return jax.shard_map(
        on_device,
        mesh=mesh,
        in_specs=(P(("groups", "blk"), None), P(("groups", "blk"))),
        out_specs=P(("groups", "blk"), None, None, None),
        check_vma=False,
    )
```

```python
import functools
import math

import jax
import jax.numpy as jnp
import numpy as np
from jax import lax
from jax.experimental import pallas as pl
from jax.experimental.pallas import tpu as pltpu
from jax.sharding import PartitionSpec as P

NWIN = 8
WS = 12000
F = 512
LOWBIN = 60
LAG = 400
HOPS = 3
NLAG = 2 * LAG + 1
QUARTER = WS // 4
ENDS = (512, 1536, QUARTER)
PADDED = -(-QUARTER // 128) * 128
PLUS = 384
LANES = 512
FOURTH = F // 4
BINS = np.concatenate([LOWBIN + np.arange((m - LOWBIN) % 4, F, 4) for m in (0, 2, 1, 3)])
PACK = 4
TAIL = 128
MIB = 1024 * 1024


def moved(block, source_of):
    count = lax.axis_size("blk")
    return lax.ppermute(block, "blk", [(source_of(i) % count, i) for i in range(count)])


def inverse_table():
    bin_index = jnp.asarray(BINS, jnp.int32)[:, None]
    lag_index = jnp.arange(LANES, dtype=jnp.int32)[None, :] - (LAG - PLUS) + WS
    residue = (bin_index * lag_index % WS).astype(jnp.float32)
    angles = 2.0 * math.pi / WS * residue
    return jnp.cos(angles).astype(jnp.bfloat16), (-jnp.sin(angles)).astype(jnp.bfloat16)


def forward_table():
    angles = 2.0 * np.pi / WS * (BINS[:, None] * np.arange(QUARTER)[None, :] % WS)
    even, odd = np.split(angles, 2)
    table = np.zeros((2 * F, PADDED), np.float32)
    table[:, :QUARTER] = np.concatenate([np.cos(even), -np.sin(even), np.cos(odd), -np.sin(odd)])
    return table.astype(jnp.bfloat16)


def spectrum_kernel(capacity, id_ref, x_ref, table_ref, out_ref, samples, table, even, odd, sems):
    begins = (0,) + ENDS[:-1]
    copies = []
    for c, (begin, end) in enumerate(zip(begins, ENDS)):
        lanes = slice(begin, end if end < QUARTER else PADDED)
        pairs = [(table_ref.at[:, lanes], table.at[:, lanes])]
        for j in range(4):
            source = x_ref.at[j * QUARTER + begin : j * QUARTER + end, :]
            pairs.append((source, samples.at[j, begin:end, :]))
        copies.append(
            [pltpu.make_async_copy(a, b, sems.at[c, i]) for i, (a, b) in enumerate(pairs)]
        )
    for group in copies:
        for copy in group:
            copy.start()
    rec_count = id_ref.shape[1]
    ids = id_ref[...]
    owner = ids // rec_count
    row = jnp.broadcast_to(owner, (rec_count, rec_count))
    before = lax.broadcasted_iota(jnp.int32, row.shape, 0) < lax.broadcasted_iota(
        jnp.int32, row.shape, 1
    )
    rank = jnp.sum(jnp.where((row == row.T) & before, 1, 0), axis=0, keepdims=True)
    target = owner * capacity + rank
    label = (ids % rec_count + 1).astype(jnp.float32)
    out_rows = out_ref.shape[0]
    slot = lax.broadcasted_iota(jnp.int32, (out_rows, rec_count), 0) * PACK
    lane = lax.broadcasted_iota(jnp.int32, (out_rows, TAIL), 1)
    labels = jnp.zeros((out_rows, TAIL), jnp.float32)
    picks = []
    for q in range(PACK):
        hit = slot + q == target
        labels = jnp.where(
            lane == q, jnp.sum(jnp.where(hit, label, 0.0), axis=1, keepdims=True), labels
        )
        picks.append(jnp.where(hit, 1.0, 0.0).astype(jnp.bfloat16))
    pick = jnp.concatenate(picks)
    out_ref[:, PACK * 2 * F :] = labels.astype(jnp.bfloat16)
    for group, begin, end in zip(copies, begins, ENDS):
        for copy in group:
            copy.wait()
        for turn, total in enumerate((even, odd)):
            rows = slice(turn * F, (turn + 1) * F)
            parts = [
                jnp.dot(
                    table[rows, begin:end],
                    samples[j, begin:end, :],
                    preferred_element_type=jnp.float32,
                )
                for j in range(4)
            ]
            if turn == 0:
                straight, across = parts[0] + parts[2], parts[1] + parts[3]
                signs, order = (1, -1, 1, -1), (0, 1, 2, 3)
            else:
                straight, across = parts[0] - parts[2], parts[1] - parts[3]
                signs, order = (1, -1, -1, 1), (2, 3, 0, 1)
            for block in range(4):
                mine = slice(block * FOURTH, (block + 1) * FOURTH)
                theirs = slice(order[block] * FOURTH, (order[block] + 1) * FOURTH)
                both = straight[mine] + across[theirs] if signs[block] > 0 else straight[mine] - across[theirs]
                total[mine, :] = both if begin == 0 else total[mine, :] + both

    power = jnp.sum(even[...] * even[...], axis=0, keepdims=True)
    power = (power + jnp.sum(odd[...] * odd[...], axis=0, keepdims=True)) / F
    scale = lax.rsqrt(power + 1e-06)
    half = F // 2
    for place, (part, base) in enumerate(((even, 0), (odd, 0), (even, half), (odd, half))):
        white = (part[base : base + half, :] * scale).astype(jnp.bfloat16)
        moved = lax.dot_general(
            pick, white, (((1,), (1,)), ((), ())), preferred_element_type=jnp.float32
        ).astype(jnp.bfloat16)
        for q in range(PACK):
            lanes = slice(q * 2 * F + place * half, q * 2 * F + (place + 1) * half)
            out_ref[:, lanes] = moved[q * out_rows : (q + 1) * out_rows]


def spectra(traces, record_id, capacity, slots):
    rec_count = traces.shape[0]
    shape = (slots // PACK, PACK * 2 * F + TAIL)
    return pl.pallas_call(
        functools.partial(spectrum_kernel, capacity),
        in_specs=[
            pl.BlockSpec(memory_space=pltpu.VMEM),
            pl.BlockSpec(memory_space=pl.ANY),
            pl.BlockSpec(memory_space=pl.ANY),
        ],
        out_specs=pl.BlockSpec(memory_space=pltpu.VMEM),
        out_shape=jax.ShapeDtypeStruct(shape, jnp.bfloat16),
        scratch_shapes=[
            pltpu.VMEM((4, QUARTER, rec_count), jnp.bfloat16),
            pltpu.VMEM((2 * F, PADDED), jnp.bfloat16),
            pltpu.VMEM((F, rec_count), jnp.float32),
            pltpu.VMEM((F, rec_count), jnp.float32),
            pltpu.SemaphoreType.DMA((len(ENDS), 5)),
        ],
        compiler_params=pltpu.CompilerParams(vmem_limit_bytes=56 * MIB),
        cost_estimate=pl.CostEstimate(
            flops=4 * rec_count * WS * F, bytes_accessed=2 * WS * (rec_count + F), transcendentals=0
        ),
        name="spectra",
    )(record_id.reshape(1, rec_count), traces.T, jnp.asarray(forward_table()))


def place_kernel(arrived_ref, out_ref, *half_refs):
    rec_count = out_ref.shape[0]
    rows = arrived_ref.shape[0]
    side = rec_count // NWIN // 2
    labels = arrived_ref[:, PACK * 2 * F :].astype(jnp.float32).T.astype(jnp.int32) - 1
    want = lax.broadcasted_iota(jnp.int32, (rec_count, rows), 0)
    total = None
    for q in range(PACK):
        label = labels[q : q + 1, :]
        channel, window = label // NWIN, label % NWIN
        row = (channel // side * NWIN + window) * side + channel % side
        pick = jnp.where(want == jnp.where(label >= 0, row, -1), 1.0, 0.0).astype(jnp.bfloat16)
        part = jnp.dot(
            pick,
            arrived_ref[:, q * 2 * F : (q + 1) * 2 * F],
            preferred_element_type=jnp.float32,
        )
        total = part if q == 0 else total + part
    panel = total.astype(jnp.bfloat16)
    out_ref[...] = panel
    for half, ref in enumerate(half_refs):
        ref[...] = panel[half * rec_count // 2 : (half + 1) * rec_count // 2]


def place(arrived, rec_count):
    return pl.pallas_call(
        place_kernel,
        out_shape=[
            jax.ShapeDtypeStruct((rows, 2 * F), jnp.bfloat16)
            for rows in (rec_count,)
        ],
        compiler_params=pltpu.CompilerParams(vmem_limit_bytes=8 * MIB),
        name="place",
    )(arrived)


def correlate_kernel(own_pair, spans, group, batch, count, *refs):
    hop_ref, own_ref = refs[:2]
    other_refs = refs[2 : 2 + count]
    cos_ref, sin_ref = refs[2 + count : 4 + count]
    out_ref, mine, theirs, cross, done, sems = refs[-6:]
    full = mine.shape[1] // NWIN
    side = full // 2
    width = theirs.shape[1] // NWIN
    own_blocks = [(own_ref, half * NWIN * side, half * side) for half in range(2)]
    if len(other_refs) * side < width:
        blocks = [(other_refs[0], half * NWIN * side, half * side) for half in range(2)]
    else:
        blocks = [(ref, 0, half * side) for half, ref in enumerate(other_refs)]
    for w in range(NWIN):
        for ref, base, place in own_blocks:
            source = slice(base + w * side, base + (w + 1) * side)
            rows = slice(w * full + place, w * full + place + side)
            real = ref[source, :F].astype(jnp.float32)
            imag = ref[source, F:].astype(jnp.float32)
            mine[0, rows, :] = real + imag
            mine[1, rows, :] = real
            mine[2, rows, :] = imag
        for ref, base, place in blocks:
            source = slice(base + w * side, base + (w + 1) * side)
            rows = slice(w * width + place, w * width + place + side)
            real = ref[source, :F].astype(jnp.float32)
            imag = ref[source, F:].astype(jnp.float32)
            theirs[0, rows, :] = real
            theirs[1, rows, :] = real + imag
            theirs[2, rows, :] = real - imag

    shared = 4

    def channels_from(step, carry):
        blocks = [
            pl.ds(pl.multiple_of(w * full + step * group, group), group) for w in range(NWIN)
        ]
        for tile in range(F // 128):
            lanes = slice(tile * 128, (tile + 1) * 128)
            for first in range(0, group, shared):
                total = [[None] * 3 for _ in range(shared)]
                for w in range(NWIN):
                    for j in range(3):
                        factor = theirs[j, w * width : (w + 1) * width, lanes]
                        rows = mine.at[j, blocks[w], lanes]
                        for c in range(shared):
                            term = factor * rows[first + c : first + c + 1, :]
                            total[c][j] = term if w == 0 else total[c][j] + term
                for c in range(shared):
                    rows = pl.ds(
                        pl.multiple_of((step * group + first + c) * width, width), width
                    )
                    cross[rows, tile * 128 : (tile + 1) * 128] = (
                        total[c][0] - total[c][2]
                    ).astype(jnp.bfloat16)
                    cross[rows, F + tile * 128 : F + (tile + 1) * 128] = (
                        total[c][0] - total[c][1]
                    ).astype(jnp.bfloat16)
        return carry

    lax.fori_loop(0, full // group, channels_from, 0)
    unit = 1.0 / math.sqrt(F * NWIN)
    copies = []
    for step in range(full // batch):
        mine_rows = slice(step * batch * width, (step + 1) * batch * width)
        even = jnp.dot(cross[mine_rows, :F], cos_ref[...], preferred_element_type=jnp.float32)
        uneven = jnp.dot(cross[mine_rows, F:], sin_ref[...], preferred_element_type=jnp.float32)
        later = (even + uneven) * unit
        earlier = (even - uneven) * unit
        lane = lax.broadcasted_iota(jnp.int32, (batch * width, 128), 1)
        last = (2 * LAG - PLUS) % 128
        mirror = (last - lane) & 127
        turned = [
            jnp.take_along_axis(earlier[:, q * 128 : (q + 1) * 128], mirror, axis=1)
            for q in range(LANES // 128)
        ]
        top = (2 * LAG - PLUS) // 128
        pieces = [
            jnp.where(lane <= last, turned[top - t], turned[top - 1 - t]) for t in range(PLUS // 128)
        ]
        lagged = jnp.concatenate(pieces + [later[:, : NLAG - PLUS]], axis=1)
        lagged = lagged.reshape(batch, width, NLAG)
        if own_pair:
            channel = lax.broadcasted_iota(jnp.int32, lagged.shape, 0) + step * batch
            partner = lax.broadcasted_iota(jnp.int32, lagged.shape, 1) + spans[0][1]
            lagged = jnp.where(channel == partner, 0.0, lagged)
        channels = slice(step * batch, (step + 1) * batch)
        done[channels] = lagged.astype(jnp.bfloat16)
        for k, (hop, begin, start, length) in enumerate(spans):
            copy = pltpu.make_async_copy(
                done.at[channels, start : start + length],
                out_ref.at[channels, hop_ref[0] if hop is None else hop, begin : begin + length],
                sems.at[step, k],
            )
            copy.start()
            copies.append(copy)
    for copy in copies:
        copy.wait()


def correlate(own, others, inverse, hop, spans, result, own_pair=False):
    rows = sum(other.shape[0] for other in others)
    width = rows // NWIN
    full = own.shape[0] // NWIN
    group = 8
    batch = 128 // width
    operands = [jnp.asarray(hop, jnp.int32).reshape(1), own, *others, *inverse]
    in_specs = [pl.BlockSpec(memory_space=pltpu.SMEM)]
    in_specs += [pl.BlockSpec(memory_space=pltpu.VMEM)] * (len(operands) - 1)
    aliases = {}
    if result is not None:
        in_specs.append(pl.BlockSpec(memory_space=pl.ANY))
        aliases = {len(operands): 0}
        operands.append(result)
    pairs = full * width
    return pl.pallas_call(
        functools.partial(correlate_kernel, own_pair, spans, group, batch, len(others)),
        in_specs=in_specs,
        out_specs=pl.BlockSpec(memory_space=pl.ANY),
        out_shape=jax.ShapeDtypeStruct((full, HOPS + 1, full, NLAG), jnp.bfloat16),
        scratch_shapes=[
            pltpu.VMEM((3, own.shape[0], F), jnp.float32),
            pltpu.VMEM((3, rows, F), jnp.float32),
            pltpu.VMEM((pairs, 2 * F), jnp.bfloat16),
            pltpu.VMEM((full, width, NLAG), jnp.bfloat16),
            pltpu.SemaphoreType.DMA((full // batch, len(spans))),
        ],
        input_output_aliases=aliases,
        compiler_params=pltpu.CompilerParams(vmem_limit_bytes=24 * MIB),
        cost_estimate=pl.CostEstimate(
            flops=pairs * 2 * F * NLAG * 4, bytes_accessed=pairs * NLAG * 2, transcendentals=0
        ),
        name="correlate",
    )(*operands)


def on_device(traces, record_id):
    rec_count = traces.shape[0]
    peers = lax.axis_size("blk")
    capacity = 2 * rec_count // peers
    slots = peers * capacity
    outgoing = spectra(traces, record_id, capacity, slots)
    width = outgoing.shape[1]
    arrived = lax.all_to_all(
        outgoing.reshape(peers, capacity // PACK, width), "blk", split_axis=0, concat_axis=0, tiled=True
    )
    arrived, inverse = lax.optimization_barrier((arrived, inverse_table()))
    (own,) = place(arrived.reshape(slots // PACK, width), rec_count)

    odd = lax.axis_index("blk") % 2
    near_hop, far_hop = 1 + 2 * odd, 3 - 2 * odd
    barrier = lax.optimization_barrier
    side = rec_count // NWIN // 2
    whole, first, second = (None, 0, 0, 2 * side), (None, 0, 0, side), (None, side, 0, side)

    def add(others, hop, *spans, own_pair=False):
        return correlate(own, others, inverse, hop, spans, result, own_pair)

    result = None
    whole = (None, 0, 0, 2 * side)

    def add(others, hop, own_pair=False):
        return correlate(own, others, inverse, hop, (whole,), result, own_pair)

    result = None
    ahead = moved(own, lambda i: i + 2)
    result = add([own], 0, own_pair=True)
    again, ahead, result = barrier((own, ahead, result))
    far = moved(ahead, lambda i: i ^ 1)
    near = moved(again, lambda i: i + 3 if i % 2 else i + 1)
    result = add([ahead], 2)
    far, result = barrier((far, result))
    result = add([far], far_hop)
    near, result = barrier((near, result))
    return add([near], near_hop)


def solution(mesh):
    return jax.shard_map(
        on_device,
        mesh=mesh,
        in_specs=(P(("groups", "blk"), None), P(("groups", "blk"))),
        out_specs=P(("groups", "blk"), None, None, None),
        check_vma=False,
    )
```
